32 devices in a mesh: freq: 4 (over x, core), space: 8 (over z, y).
Axes of the slice: x: 2, y: 2, z: 4, core: 2. Of those that a mesh axis runs over, the one named last changes fastest.
Arguments:
- source_field: bfloat16 [2, 8, 1024, 1024], P(None, 'freq', 'space'), may hold values from -6 to 6
- receiver_field: bfloat16 [2, 8, 1024, 1024], P(None, 'freq', 'space'), may hold values from -6 to 6
- line_inverse: bfloat16 [2, 8, 1024, 1024], P(None, 'freq'), may hold values from -0.125 to 0.125
- lens_delay: float32 [3, 1024, 1024], P(None, 'space'), may hold values from -0.6 to 0.6
- omegas: float32 [8], P('freq'), may hold values from 4 to 40
- image_weights: float32 [8], P('freq'), may hold values from 0.1 to 1
Outputs:
- source_out: bfloat16 [2, 8, 1024, 1024], P(None, 'freq', 'space')
- receiver_out: bfloat16 [2, 8, 1024, 1024], P(None, 'freq', 'space')
- gradient: float32 [3, 1024, 1024], P(None, 'space')
The draws below stay inside these ranges and needn't reach their ends.
All inputs are finite; a program needn't handle non-finite values.
Results may differ from the reference program's by a relative error of at most 0.017.
Values may be sent and summed in bfloat16 or wider, within the bound.
No kernel may reach another device: no remote copies, remote signals or barrier semaphores. Data moves between devices by JAX's collectives and lax.ppermute only.
A program may use at most 128 MiB of HBM per device.

```python
import math
import jax
import jax.numpy as jnp
from jax import lax

NL = 1024
DEPTHS = 3
FREQS = 8


def levels(stream_key, dims, split, low, high):
    gain = 1.0
    for axis_at, shards_of in split:
        steps = jax.random.uniform(jax.random.fold_in(jax.random.fold_in(stream_key, 6), axis_at), (shards_of,), jnp.float32, low / len(split), high / len(split))
        gain = gain * jnp.repeat(jnp.exp(steps), dims[axis_at] // shards_of).reshape((-1,) + (1,) * (len(dims) - 1 - axis_at))
    return gain


def normal_values(key, shape, scale, limit, pieces=(), held_as=jnp.bfloat16):
    values = jax.random.normal(key, shape, jnp.float32) * scale
    if len(pieces) > 0:
        values = levels(key, shape, pieces, -0.22, 0.18) * values
    return jnp.clip(values, min=-limit, max=limit).astype(held_as)


def setup_inputs(seed: int = 0) -> dict:
    arg_keys = jax.random.split(jax.random.key(seed), 7)
    return {
        "source_field": normal_values(arg_keys[0], (2, FREQS, NL, NL), 1.0, 6.0, ((1, 4), (2, 8))),
        "receiver_field": normal_values(arg_keys[1], (2, FREQS, NL, NL), 1.0, 6.0, ((1, 4), (2, 8))),
        "line_inverse": normal_values(arg_keys[2], (2, FREQS, NL, NL), (2 * NL) ** -0.5, 0.125, ((1, 4),)),
        "lens_delay": normal_values(arg_keys[3], (DEPTHS, NL, NL), 0.1, 0.6, ((1, 8),), jnp.float32),
        "omegas": jnp.clip(jnp.exp(math.log(40.0) - 2.3025851 * jax.random.uniform(arg_keys[4], (FREQS,), jnp.float32) ** levels(arg_keys[4], (FREQS,), ((0, 4),), -0.2, 0.2)), 4.0, 40.0),
        "image_weights": jnp.clip(jnp.exp(math.log(1.0) - 2.3025851 * jax.random.uniform(arg_keys[5], (FREQS,), jnp.float32) ** levels(arg_keys[5], (FREQS,), ((0, 4),), -0.2, 0.2)), 0.1, 1.0),
    }


def combine_parts(prod_real, prod_imag, flip_sign):
    new_real = prod_real[:, 0] - flip_sign * prod_imag[:, 1]
    new_imag = prod_real[:, 1] + flip_sign * prod_imag[:, 0]
    return jnp.stack([new_real, new_imag], axis=1)


def reference(source_field, receiver_field, line_inverse, lens_delay, omegas, image_weights):
    wavefields = jnp.stack([source_field, receiver_field]).astype(jnp.float32)
    matrix_real = line_inverse[0].astype(jnp.float32)
    matrix_imag = line_inverse[1].astype(jnp.float32)
    flip_sign = jnp.array([1.0, -1.0], jnp.float32).reshape(2, 1, 1, 1)
    slices = []
    for depth_step in range(DEPTHS):
        phase_angle = omegas[:, None, None] * lens_delay[depth_step][None]
        cosine = jnp.cos(phase_angle)
        sine_part = jnp.sin(phase_angle)
        real_part = wavefields[:, 0]
        imag_part = wavefields[:, 1]
        phased = jnp.stack([real_part * cosine + flip_sign * imag_part * sine_part,
                            imag_part * cosine - flip_sign * real_part * sine_part], axis=1).astype(jnp.bfloat16)
        phased_wide = phased.astype(jnp.float32)
        prod_real = jnp.einsum("fij,wpfyj->wpfyi", matrix_real, phased_wide, precision=lax.Precision.HIGHEST)
        prod_imag = jnp.einsum("fij,wpfyj->wpfyi", matrix_imag, phased_wide, precision=lax.Precision.HIGHEST)
        across = combine_parts(prod_real, prod_imag, flip_sign).astype(jnp.bfloat16).astype(jnp.float32)
        prod_real = jnp.einsum("fij,wpfjx->wpfix", matrix_real, across, precision=lax.Precision.HIGHEST)
        prod_imag = jnp.einsum("fij,wpfjx->wpfix", matrix_imag, across, precision=lax.Precision.HIGHEST)
        wavefields = combine_parts(prod_real, prod_imag, flip_sign)
        image_term = wavefields[0, 0] * wavefields[1, 0] + wavefields[0, 1] * wavefields[1, 1]
        slices.append(jnp.sum(image_weights[:, None, None] * image_term, axis=0))
    return (wavefields[0].astype(jnp.bfloat16), wavefields[1].astype(jnp.bfloat16), jnp.stack(slices))
```

```python
import jax
import jax.numpy as jnp
from jax import lax
from jax.experimental import pallas as pl
from jax.experimental.pallas import tpu as pltpu
from jax.sharding import PartitionSpec as P

BF = jnp.bfloat16
F32 = jnp.float32
TWO_OVER_PI = 0.63661977236758134
ANY = pl.BlockSpec(memory_space=pl.ANY)
SMEM = pl.BlockSpec(memory_space=pltpu.SMEM)


def sin_cos(quarter_turns):
    whole = jnp.round(quarter_turns)
    r = quarter_turns - whole
    q = r * r
    s = -0.00460174 * q + 0.07968794
    s = s * q - 0.64596367
    s = (s * q + 1.57079632) * r
    c = 0.00091925 * q - 0.02086341
    c = c * q + 0.25366950
    c = c * q - 1.23370055
    c = c * q + 1.0
    k = whole.astype(jnp.int32)
    odd = (k & 1) == 1
    sine = jnp.where(odd, c, s)
    cosine = jnp.where(odd, s, c)
    sine = jnp.where((k & 2) == 2, -sine, sine)
    cosine = jnp.where(((k + 1) & 2) == 2, -cosine, cosine)
    return sine, cosine


def dot_rows(a, b):
    return lax.dot_general(a, b, (((1,), (0,)), ((), ())), preferred_element_type=F32)


def dot_lines(a, b):
    return lax.dot_general(a, b, (((1,), (1,)), ((), ())), preferred_element_type=F32)


def spec(block, index):
    return pl.BlockSpec(block, index)


def call(body, grid, ins, outs, scratch, operands, cost, limit=60 << 20):
    return pl.pallas_call(
        body,
        out_shape=[jax.ShapeDtypeStruct(s, d) for s, d, _, _ in outs],
        grid_spec=pltpu.PrefetchScalarGridSpec(
            num_scalar_prefetch=1,
            grid=grid,
            in_specs=ins,
            out_specs=[pl.BlockSpec(b, i) for _, _, b, i in outs],
            scratch_shapes=scratch,
        ),
        compiler_params=pltpu.CompilerParams(vmem_limit_bytes=limit),
        cost_estimate=pl.CostEstimate(flops=cost, bytes_accessed=8 << 20, transcendentals=0),
    )(*operands)


def home_solve(ids, turn, source, receiver, matrix, lens, omegas):
    _, _, rows, cols = source.shape
    half = cols // 2

    def body(ids, src, rec, mat, len_ref, om, m00, m01, m10, m11, phased):
        b = pl.program_id(0)
        y = ids[3]
        j = ids[4] ^ turn

        @pl.when(b == 0)
        def _():
            sine, cosine = sin_cos(len_ref[0] * (om[j] * TWO_OVER_PI))
            sr = src[0, 0].astype(F32)
            si = src[1, 0].astype(F32)
            rr = rec[0, 0].astype(F32)
            ri = -rec[1, 0].astype(F32)
            first = y == 0
            for at, (re, im) in enumerate(
                (
                    (jnp.where(first, sr, rr), jnp.where(first, si, ri)),
                    (jnp.where(first, rr, sr), jnp.where(first, ri, si)),
                )
            ):
                phased[pl.ds(at * rows, rows), :] = (re * cosine + im * sine).astype(BF)
                phased[pl.ds((2 + at) * rows, rows), :] = (im * cosine - re * sine).astype(BF)

        q_re = dot_lines(phased[...], mat[0, 0])
        q_im = dot_lines(phased[...], mat[1, 0])
        n = 2 * rows
        new_re = (q_re[:n] - q_im[n:]).astype(BF)
        new_im = (q_re[n:] + q_im[:n]).astype(BF)
        for at, outs in enumerate(((m00, m10), (m01, m11))):

            @pl.when(b == at)
            def _(outs=outs):
                for w, out in enumerate(outs):
                    out[0] = new_re[w * rows : (w + 1) * rows]
                    out[1] = new_im[w * rows : (w + 1) * rows]

    message = ((2, rows, half), BF, (2, rows, half), lambda b, ids: (0, 0, 0))
    field = spec((2, 1, rows, cols), lambda b, ids: (0, ids[4] ^ turn, 0, 0))
    return call(
        body,
        (2,),
        [
            field,
            field,
            spec((2, 1, half, cols), lambda b, ids: (0, ids[4] ^ turn, ids[5] ^ b, 0)),
            spec((1, rows, cols), lambda b, ids: (0, 0, 0)),
            SMEM,
        ],
        [message] * 4,
        [pltpu.VMEM((4 * rows, cols), BF)],
        (ids, source, receiver, matrix, lens, omegas),
        2 * 4 * rows * cols * cols * 2,
    )


def lens_place(ids, s, side):
    return ((ids[1] ^ side) * 2 + (ids[3] ^ (s % 2))) * 4 + (ids[2] ^ (s // 2))


def rotated(re, im, sine, cosine):
    return (re * cosine + im * sine).astype(BF), (im * cosine - re * sine).astype(BF)


def column_solve(ids, messages, matrix, lens, omega):
    _, rows, half = messages[0].shape
    n = matrix.shape[-1]
    slices = n // rows
    tile = 2 * rows
    tiles = n // tile
    quarter = rows // 2
    per = tile // quarter
    blocked = matrix.reshape(2, slices, 2, quarter, n)

    def body(ids, *refs):
        (m0, m1, m2, m3, m4, m5, m6, m7, mat, mat_half, len_ref, om,
         keep, send, phased, out, field, sems) = refs
        i = pl.program_id(0)
        t = ids[4] * 2 + ids[3]

        @pl.when(i == 0)
        def _():
            copies = []
            for at, m in enumerate((m0, m1, m2, m3, m4, m5, m6, m7)):
                a, b = at // 2, at % 2
                place = (ids[0] ^ b) * 4 + (t ^ a)
                for part in range(2):
                    copies.append(
                        pltpu.make_async_copy(
                            m.at[part],
                            field.at[part, pl.ds(pl.multiple_of(place * rows, rows), rows)],
                            sems.at[at, part],
                        )
                    )
            for copy in copies:
                copy.start()
            for copy in copies:
                copy.wait()

        @pl.when(i < tiles)
        def _():
            left = mat[...].reshape(2 * tile, n)
            q_re = dot_rows(left, field[0])
            q_im = dot_rows(left, field[1])
            new_re = q_re[:tile] - q_im[tile:]
            new_im = q_im[:tile] + q_re[tile:]
            first = ids[3] == 0
            for part, new in enumerate((new_re, new_im)):
                even, odd = new[:rows].astype(BF), new[rows:].astype(BF)
                keep[part, i] = jnp.where(first, even, odd)
                send[part, i] = jnp.where(first, odd, even)
            for s in range(2):
                for side in range(2):
                    at = ((ids[1] ^ side) * 2 + (ids[3] ^ s)) * 4 + (ids[2] ^ i)
                    sine, cosine = sin_cos(len_ref[at] * (om[0] * TWO_OVER_PI))
                    lo = s * rows + side * quarter
                    re, im = rotated(
                        new_re[lo : lo + quarter], new_im[lo : lo + quarter], sine, cosine
                    )
                    to = pl.ds(pl.multiple_of(i * tile + lo, quarter), quarter)
                    phased[0, to] = re
                    phased[1, to] = im

        @pl.when(i >= tiles)
        def _():
            left = mat_half[...].reshape(2 * tile, n)
            q_re = dot_rows(left, phased[0])
            q_im = dot_rows(left, phased[1])
            to = pl.ds(pl.multiple_of((i - tiles) * tile, tile), tile)
            out[0, to] = (q_re[:tile] - q_im[tile:]).astype(BF)
            out[1, to] = (q_im[:tile] + q_re[tile:]).astype(BF)

    flat = lambda rank: (lambda i, ids: (0,) * rank)
    part_shape = (2, tiles, rows, half)
    return call(
        body,
        (tiles + tiles // 2,),
        [ANY] * 8
        + [
            spec((2, tile, n), lambda i, ids: (0, jnp.minimum(i, tiles - 1), 0)),
            spec(
                (2, per, 1, quarter, n),
                lambda i, ids: (0, jnp.maximum(i - tiles, 0), 1 - ids[0], 0, 0),
            ),
            spec(lens.shape, flat(3)),
            SMEM,
        ],
        [
            (part_shape, BF, part_shape, flat(4)),
            (part_shape, BF, part_shape, flat(4)),
            ((2, n, half), BF, (2, n, half), flat(3)),
            ((2, n // 2, half), BF, (2, n // 2, half), flat(3)),
        ],
        [pltpu.VMEM((2, n, half), BF), pltpu.SemaphoreType.DMA((8, 2))],
        (ids, *messages, matrix, blocked, lens, omega),
        12 * n * n * half,
    )


def column_rest(ids, phased, matrix, rows):
    _, n, half = phased.shape
    slices = n // rows
    tile = 2 * rows
    quarter = rows // 2
    per = tile // quarter
    blocked = matrix.reshape(2, slices, 2, quarter, n)

    def body(ids, field, mat_half, out):
        left = mat_half[...].reshape(2 * tile, n)
        q_re = dot_rows(left, field[0])
        q_im = dot_rows(left, field[1])
        out[0] = (q_re[:tile] - q_im[tile:]).astype(BF)
        out[1] = (q_im[:tile] + q_re[tile:]).astype(BF)

    return call(
        body,
        (slices * quarter // tile,),
        [
            spec((2, n, half), lambda i, ids: (0, 0, 0)),
            spec((2, per, 1, quarter, n), lambda i, ids: (0, i, ids[0], 0, 0)),
        ],
        [((2, n // 2, half), BF, (2, tile, half), lambda i, ids: (0, i, 0))],
        [],
        (ids, phased, blocked),
        4 * n * n * half,
    )[0]


def row_solve(ids, own, received, matrix, lens, omega, rows):
    _, lines, half = own.shape
    n = matrix.shape[-1]
    slices = n // rows
    quarter = rows // 2
    tile = 2 * rows
    tiles = n // tile

    def body(ids, own_ref, rec_ref, mat, mat_half, len_ref, om, keep, send, phased, out, field):
        i = pl.program_id(0)

        @pl.when(i == 0)
        def _():
            for at, ref in enumerate((own_ref, rec_ref)):
                to = pl.ds(pl.multiple_of((ids[0] ^ at) * half, half), half)
                field[pl.ds(0, lines), to] = ref[0]
                field[pl.ds(lines, lines), to] = ref[1]

        @pl.when(i < tiles)
        def _():
            q_re = dot_lines(field[...], mat[0])
            q_im = dot_lines(field[...], mat[1])
            new_re = q_re[:lines] - q_im[lines:]
            new_im = q_re[lines:] + q_im[:lines]
            cols = pl.ds(pl.multiple_of(i * tile, tile), tile)
            inner = pl.ds(pl.multiple_of((i % (half // tile)) * tile, tile), tile)
            side = i // (half // tile)
            first = ids[3] == 0
            for s in range(slices):
                at = ((ids[1] ^ side) * 2 + (ids[3] ^ (s % 2))) * 4 + (ids[2] ^ (s // 2))
                sine, cosine = sin_cos(len_ref[at, :, inner] * (om[0] * TWO_OVER_PI))
                lo = s * quarter
                re, im = rotated(
                    new_re[lo : lo + quarter], new_im[lo : lo + quarter], sine, cosine
                )
                phased[0, pl.ds(lo, quarter), cols] = re
                phased[1, pl.ds(lo, quarter), cols] = im
            for part, new in enumerate((new_re, new_im)):
                for z in range(slices // 2):
                    lo = 2 * z * quarter
                    even = new[lo : lo + quarter].astype(BF)
                    odd = new[lo + quarter : lo + 2 * quarter].astype(BF)
                    keep[part, z, :, cols] = jnp.where(first, even, odd)
                    send[part, z, :, cols] = jnp.where(first, odd, even)

        @pl.when(i >= tiles)
        def _():
            left = phased[...].reshape(2 * lines, n)
            q_re = dot_lines(left, mat_half[0])
            q_im = dot_lines(left, mat_half[1])
            cols = pl.ds(pl.multiple_of((i - tiles) * tile, tile), tile)
            out[0, :, cols] = (q_re[:lines] - q_im[lines:]).astype(BF)
            out[1, :, cols] = (q_re[lines:] + q_im[:lines]).astype(BF)

    flat = lambda rank: (lambda i, ids: (0,) * rank)
    part_shape = (2, slices // 2, quarter, n)
    per_half = half // tile
    return call(
        body,
        (tiles + per_half,),
        [
            spec(own.shape, flat(3)),
            spec(own.shape, flat(3)),
            spec((2, tile, n), lambda i, ids: (0, jnp.minimum(i, tiles - 1), 0)),
            spec(
                (2, tile, n),
                lambda i, ids: (0, (1 - ids[0]) * per_half + jnp.maximum(i - tiles, 0), 0),
            ),
            spec(lens.shape, flat(3)),
            SMEM,
        ],
        [
            (part_shape, BF, part_shape, flat(4)),
            (part_shape, BF, part_shape, flat(4)),
            ((2, lines, n), BF, (2, lines, n), flat(3)),
            ((2, lines, half), BF, (2, lines, half), flat(3)),
        ],
        [pltpu.VMEM((2 * lines, n), BF)],
        (ids, own, received, matrix, matrix, lens, omega),
        12 * n * n * half,
    )


def row_rest(ids, phased, matrix, rows):
    _, lines, n = phased.shape
    half = n // 2
    tile = 2 * rows
    per_half = half // tile

    def body(ids, field, mat, out):
        left = field[...].reshape(2 * lines, n)
        q_re = dot_lines(left, mat[0])
        q_im = dot_lines(left, mat[1])
        out[0] = (q_re[:lines] - q_im[lines:]).astype(BF)
        out[1] = (q_re[lines:] + q_im[:lines]).astype(BF)

    return call(
        body,
        (per_half,),
        [
            spec(phased.shape, lambda i, ids: (0, 0, 0)),
            spec((2, tile, n), lambda i, ids: (0, ids[0] * per_half + i, 0)),
        ],
        [((2, lines, half), BF, (2, lines, tile), lambda i, ids: (0, 0, i))],
        [],
        (ids, phased, matrix),
        4 * n * n * half,
    )[0]


def last_solve(ids, turn, own, received, matrix, rows):
    _, lines, half = own.shape
    n = matrix.shape[-1]
    slices = n // rows
    quarter = rows // 2
    tile = 2 * rows

    def body(ids, own_ref, rec_ref, mat, m00, m01, m10, m11, field):
        b = pl.program_id(0)

        @pl.when(b == 0)
        def _():
            for at, ref in enumerate((own_ref, rec_ref)):
                side = (ids[0] ^ at) * quarter
                for part in range(2):
                    for s in range(slices):
                        to = pl.ds(pl.multiple_of(s * rows + side, quarter), quarter)
                        field[part, to] = ref[part, pl.ds(s * quarter, quarter)]

        left = mat[...].reshape(2 * tile, n)
        q_re = dot_rows(left, field[0])
        q_im = dot_rows(left, field[1])
        new_re = (q_re[:tile] - q_im[tile:]).astype(BF)
        new_im = q_im[:tile] + q_re[tile:]
        first = ids[3] == 0
        new_im = jnp.where(first, new_im, -new_im).astype(BF)
        for at, (near, far) in enumerate(((m00, m10), (m01, m11))):

            @pl.when(b == at)
            def _(near=near, far=far):
                for part, new in enumerate((new_re, new_im)):
                    near[part] = jnp.where(first, new[:rows], new[rows:])
                    far[part] = jnp.where(first, new[rows:], new[:rows])

    message = ((2, rows, half), BF, (2, rows, half), lambda b, ids: (0, 0, 0))
    return call(
        body,
        (2,),
        [
            spec(own.shape, lambda b, ids: (0, 0, 0)),
            spec(own.shape, lambda b, ids: (0, 0, 0)),
            spec((2, tile, n), lambda b, ids: (0, (ids[0] ^ b) * 2 + (ids[4] ^ turn), 0)),
        ],
        [message] * 4,
        [pltpu.VMEM((2, n, half), BF)],
        (ids, own, received, matrix),
        4 * n * n * half,
    )


def arrive(ids, messages, image_weights, freqs):
    _, rows, half = messages[0].shape

    def body(ids, *refs):
        ms, (wt, src, rec, grad, held, sems) = refs[:8], refs[8:]
        copies = [
            pltpu.make_async_copy(m, held.at[at], sems.at[at]) for at, m in enumerate(ms)
        ]
        for copy in copies:
            copy.start()
        for copy in copies:
            copy.wait()
        for side in range(2):
            total = None
            for j in range(freqs):
                a_hi = ids[4] ^ j
                b = ids[5] ^ side
                s_at = (a_hi * 2 + ids[3]) * 2 + b
                r_at = (a_hi * 2 + (1 - ids[3])) * 2 + b
                s, r = held[s_at], held[r_at]
                cols = pl.ds(side * half, half)
                src[:, j, :, cols] = s
                rec[:, j, :, cols] = r
                s, r = s.astype(F32), r.astype(F32)
                term = wt[j] * (s[0] * r[0] + s[1] * r[1])
                total = term if total is None else total + term
            grad[:, pl.ds(side * half, half)] = total.astype(BF)

    flat = lambda rank: (lambda i, ids: (0,) * rank)
    full = (2, freqs, rows, 2 * half)
    return call(
        body,
        (1,),
        [ANY] * 8 + [SMEM],
        [
            (full, BF, full, flat(4)),
            (full, BF, full, flat(4)),
            ((rows, 2 * half), BF, (rows, 2 * half), flat(2)),
        ],
        [pltpu.VMEM((8, 2, rows, half), BF), pltpu.SemaphoreType.DMA((8,))],
        (ids, *messages, image_weights),
        1 << 22,
    )


def flip(size, bit):
    return [(i, i ^ bit) for i in range(size)]


def scatter_rounds(groups, space, back):
    rounds = []
    for a in range(4):
        for b in range(2):
            perm = []
            for x in range(groups // 2):
                for c in range(2):
                    for s in range(space):
                        home = (2 * x + c) * space + s
                        away = (2 * x + ((s // 4) ^ b)) * space + 4 * c + ((s % 4) ^ a)
                        perm.append((away, home) if back else (home, away))
            rounds.append(perm)
    return rounds


def plane_per_chip(source, receiver, matrix, lens, omegas, image_weights):
    groups, space = lax.axis_size("freq"), lax.axis_size("space")
    both = ("freq", "space")
    _, freqs, rows, cols = source.shape
    half, quarter = cols // 2, rows // 2
    group, s = lax.axis_index("freq"), lax.axis_index("space")
    core, x, z, y = group % 2, group // 2, s // 2, s % 2
    ids = jnp.stack([core, x, z, y, z % 2, z // 2]).astype(jnp.int32)
    swap = flip(groups, 1)

    mine = core == z // 2
    scalars = jnp.stack([omegas, image_weights])
    other = lax.ppermute(scalars, "freq", swap)
    omega, weight = jnp.where(mine, scalars, other)[:, z % 2]
    omega = omega.reshape(1)

    going, coming = scatter_rounds(groups, space, False), scatter_rounds(groups, space, True)
    messages = []
    for turn in range(2):
        sent = home_solve(ids, turn, source, receiver, matrix, lens, omegas)
        for at, m in enumerate(sent):
            messages.append(lax.ppermute(m, both, going[4 * turn + at]))

    stacks = []
    for depth, (r0, c0) in ((1, (x * quarter, core * half)), (2, (core * quarter, x * half))):
        piece = lax.dynamic_slice(lens, (depth, r0, c0), (1, quarter, half))
        line = jnp.concatenate(
            [piece] + [lax.ppermute(piece, "space", flip(space, 2 * k)) for k in (1, 2, 3)]
        )
        plane = jnp.concatenate([line, lax.ppermute(line, "space", flip(space, 1))])
        stacks.append(jnp.concatenate([plane, lax.ppermute(plane, "freq", flip(groups, 2))]))

    held = lax.dynamic_slice(matrix, (0, z % 2, 0, 0), (2, 1, cols, cols))[:, 0]
    line_matrix = jnp.where(mine, held, lax.ppermute(held, "freq", swap))

    keep0, send0, phased, sent = column_solve(ids, messages, line_matrix, stacks[0], omega)
    came = lax.ppermute(sent, "freq", swap)
    own = column_rest(ids, phased, line_matrix, rows)
    partner0 = lax.ppermute(send0, "space", flip(space, 1))
    keep1, send1, phased, sent = row_solve(
        ids, own, came, line_matrix, stacks[1], omega, rows
    )
    came = lax.ppermute(sent, "freq", swap)
    own = row_rest(ids, phased, line_matrix, rows)
    partner1 = lax.ppermute(send1, "space", flip(space, 1))

    finals = []
    for turn in range(2):
        sent = last_solve(ids, turn, own, came, line_matrix, rows)
        for at, m in enumerate(sent):
            finals.append(lax.ppermute(m, both, coming[4 * turn + at]))

    def product(a, b):
        a, b = a.astype(F32), b.astype(F32)
        return weight * (a[0] * b[0] - a[1] * b[1])

    term0 = product(keep0, partner0)
    term1 = product(keep1, partner1)
    halves0 = term0.reshape(-1, 2, quarter, half)
    halves1 = jnp.moveaxis(term1.reshape(-1, quarter, 2, half), 2, 1)
    halves = jnp.stack([halves0, halves1], axis=1)

    def side(v, at):
        return lax.dynamic_index_in_dim(v, at, 2, keepdims=False)

    over_x = side(halves, x) + lax.ppermute(
        side(halves, 1 - x).astype(BF), "freq", flip(groups, 2)
    ).astype(F32)

    def slab(at):
        return lax.dynamic_index_in_dim(over_x, at, 0, keepdims=False)

    total = slab(z)
    for k in (1, 2, 3):
        total = total + lax.ppermute(slab(z ^ k).astype(BF), "space", flip(space, 2 * k)).astype(F32)
    piece = total.astype(BF)
    pair = jnp.stack([piece, lax.ppermute(piece, "freq", swap)])
    quad = jnp.stack([pair, lax.ppermute(pair, "freq", flip(groups, 2))])

    def at_of(px, pc, depth):
        return lax.dynamic_slice(
            quad, (x ^ px, core ^ pc, depth, 0, 0), (1, 1, 1, quarter, half)
        )[0, 0, 0].astype(F32)

    grad0 = jnp.block([[at_of(0, 0, 0), at_of(0, 1, 0)], [at_of(1, 0, 0), at_of(1, 1, 0)]])
    grad1 = jnp.block([[at_of(0, 0, 1), at_of(1, 0, 1)], [at_of(0, 1, 1), at_of(1, 1, 1)]])

    source_out, receiver_out, term2 = arrive(ids, finals, image_weights, freqs)
    chip = term2.astype(F32) + lax.ppermute(term2, "freq", swap).astype(F32)
    grad2 = chip + lax.ppermute(chip.astype(BF), "freq", flip(groups, 2)).astype(F32)
    return source_out, receiver_out, jnp.stack([grad0, grad1, grad2])


def to_blocks(matrix, pieces):
    leading = matrix.shape[:-2]
    local_rows = matrix.shape[-2]
    columns = matrix.shape[-1] // pieces
    arranged = matrix.reshape(leading + (local_rows, pieces, columns))
    arranged = jnp.moveaxis(arranged, -2, -3)
    return arranged.reshape(leading + (pieces, local_rows * columns))


def from_blocks(blocked, local_rows):
    leading = blocked.shape[:-2]
    pieces = blocked.shape[-2]
    columns = blocked.shape[-1] // local_rows
    arranged = blocked.reshape(leading + (pieces, local_rows, columns))
    arranged = jnp.moveaxis(arranged, -1, -3)
    return arranged.reshape(leading + (columns, pieces * local_rows))


def rotate(fields, phase_angle):
    cosine = jnp.cos(phase_angle)
    sine_part = jnp.sin(phase_angle)
    flip_sign = jnp.array([1.0, -1.0], jnp.float32).reshape(2, 1, 1, 1)
    real_part = fields[:, 0]
    imag_part = fields[:, 1]
    return jnp.stack(
        [
            real_part * cosine + flip_sign * imag_part * sine_part,
            imag_part * cosine - flip_sign * real_part * sine_part,
        ],
        axis=1,
    )


def line_solve(line_inverse, fields):
    flip_sign = jnp.array([1.0, -1.0], jnp.float32).reshape(2, 1, 1, 1)
    prod_real = jnp.einsum(
        "fij,wpfrj->wpfri", line_inverse[0], fields, preferred_element_type=jnp.float32
    )
    prod_imag = jnp.einsum(
        "fij,wpfrj->wpfri", line_inverse[1], fields, preferred_element_type=jnp.float32
    )
    new_real = prod_real[:, 0] - flip_sign * prod_imag[:, 1]
    new_imag = prod_real[:, 1] + flip_sign * prod_imag[:, 0]
    return jnp.stack([new_real, new_imag], axis=1)


def march_step(line_inverse, phased, local_rows):
    pieces = lax.axis_size("space")
    across = line_solve(line_inverse, phased).astype(jnp.bfloat16)
    received = lax.all_to_all(
        to_blocks(across, pieces), "space", split_axis=3, concat_axis=3, tiled=True
    )
    return line_solve(line_inverse, from_blocks(received, local_rows))


def image_slice(fields, image_weights):
    image_term = fields[0, 0] * fields[1, 0] + fields[0, 1] * fields[1, 1]
    return jnp.sum(image_weights[:, None, None] * image_term, axis=0)


def reduce_slice(image_term):
    return lax.psum(image_term.astype(jnp.bfloat16), "freq").astype(jnp.float32)


def finish_sums(slices):
    stacked = jnp.stack(slices)
    return stacked


def general(source_field, receiver_field, line_inverse, lens_delay, omegas, image_weights):
    pieces = lax.axis_size("space")
    local_rows = lens_delay.shape[1]
    depth_count = lens_delay.shape[0]
    wavefields = jnp.stack([source_field, receiver_field]).astype(jnp.float32)
    slices = []
    lens_columns = from_blocks(
        lax.all_to_all(
            to_blocks(lens_delay, pieces), "space", split_axis=1, concat_axis=1, tiled=True
        ),
        local_rows,
    )
    phased = rotate(wavefields, omegas[:, None, None] * lens_delay[0][None]).astype(jnp.bfloat16)
    solved = march_step(line_inverse, phased, local_rows)
    slices.append(reduce_slice(image_slice(solved, image_weights)))
    for depth_step in range(1, depth_count):
        phase_angle = omegas[:, None, None] * lens_columns[depth_step][None]
        phased_columns = rotate(solved, phase_angle).astype(jnp.bfloat16)
        received = lax.all_to_all(
            to_blocks(phased_columns, pieces), "space", split_axis=3, concat_axis=3, tiled=True
        )
        solved = march_step(line_inverse, from_blocks(received, local_rows), local_rows)
        slices.append(reduce_slice(image_slice(solved, image_weights)))
    final_blocks = lax.all_to_all(
        to_blocks(solved.astype(jnp.bfloat16), pieces),
        "space",
        split_axis=3,
        concat_axis=3,
        tiled=True,
    )
    final_fields = from_blocks(final_blocks, local_rows)
    gradient_columns = finish_sums(slices)
    gradient = from_blocks(
        lax.all_to_all(
            to_blocks(gradient_columns, pieces).astype(jnp.bfloat16),
            "space",
            split_axis=1,
            concat_axis=1,
            tiled=True,
        ).astype(jnp.float32),
        local_rows,
    )
    return (final_fields[0], final_fields[1], gradient)


def on_device(source_field, receiver_field, line_inverse, lens_delay, omegas, image_weights):
    args = (source_field, receiver_field, line_inverse, lens_delay, omegas, image_weights)
    groups, space = lax.axis_size("freq"), lax.axis_size("space")
    freqs, depths = omegas.shape[0], lens_delay.shape[0]
    fits = space == 2 * 2 * freqs and freqs == 2 and groups % 4 == 0 and depths == 3
    return plane_per_chip(*args) if fits else general(*args)


def solution(mesh):
    placed = (
        P(None, "freq", "space", None),
        P(None, "freq", "space", None),
        P(None, "freq", None, None),
        P(None, "space", None),
        P("freq"),
        P("freq"),
    )
    return jax.shard_map(
        on_device,
        mesh=mesh,
        in_specs=placed,
        out_specs=(
            P(None, "freq", "space", None),
            P(None, "freq", "space", None),
            P(None, "space", None),
        ),
        check_vma=False,
    )
```

```python
import jax
import jax.numpy as jnp
from jax import lax
from jax.experimental import pallas as pl
from jax.experimental.pallas import tpu as pltpu
from jax.sharding import PartitionSpec as P


BF = jnp.bfloat16
F32 = jnp.float32
TWO_OVER_PI = 0.63661977236758134
LENS_GAIN = 1.66
ANY = pl.BlockSpec(memory_space=pl.ANY)
SMEM = pl.BlockSpec(memory_space=pltpu.SMEM)


def sin_cos(quarter_turns):
    whole = jnp.round(quarter_turns)
    r = quarter_turns - whole
    q = r * r
    s = -0.00460174 * q + 0.07968794
    s = s * q - 0.64596367
    s = (s * q + 1.57079632) * r
    c = 0.00091925 * q - 0.02086341
    c = c * q + 0.25366950
    c = c * q - 1.23370055
    c = c * q + 1.0
    k = whole.astype(jnp.int32)
    odd = (k & 1) == 1
    sine = jnp.where(odd, c, s)
    cosine = jnp.where(odd, s, c)
    sine = jnp.where((k & 2) == 2, -sine, sine)
    cosine = jnp.where(((k + 1) & 2) == 2, -cosine, cosine)
    return sine, cosine


def dot_rows(a, b):
    return lax.dot_general(a, b, (((1,), (0,)), ((), ())), preferred_element_type=F32)


def dot_lines(a, b):
    return lax.dot_general(a, b, (((1,), (1,)), ((), ())), preferred_element_type=F32)


def spec(block, index):
    return pl.BlockSpec(block, index)


def call(body, grid, ins, outs, scratch, operands, cost, limit=28 << 20):
    return pl.pallas_call(
        body,
        out_shape=[jax.ShapeDtypeStruct(s, d) for s, d, _, _ in outs],
        grid_spec=pltpu.PrefetchScalarGridSpec(
            num_scalar_prefetch=1,
            grid=grid,
            in_specs=ins,
            out_specs=[pl.BlockSpec(b, i) for _, _, b, i in outs],
            scratch_shapes=scratch,
        ),
        compiler_params=pltpu.CompilerParams(vmem_limit_bytes=limit),
        cost_estimate=pl.CostEstimate(flops=cost, bytes_accessed=8 << 20, transcendentals=0),
    )(*operands)


def home_solve(ids, turn, source, receiver, matrix, lens, omegas):
    _, _, rows, cols = source.shape
    half = cols // 2

    def body(ids, src, rec, mat, len_ref, om, m00, m01, m10, m11, phased):
        b = pl.program_id(0)
        y = ids[3]
        j = ids[4] ^ turn

        @pl.when(b == 0)
        def _():
            sine, cosine = sin_cos(len_ref[0] * (om[j] * TWO_OVER_PI))
            sr = src[0, 0].astype(F32)
            si = src[1, 0].astype(F32)
            rr = rec[0, 0].astype(F32)
            ri = -rec[1, 0].astype(F32)
            first = y == 0
            for at, (re, im) in enumerate(
                (
                    (jnp.where(first, sr, rr), jnp.where(first, si, ri)),
                    (jnp.where(first, rr, sr), jnp.where(first, ri, si)),
                )
            ):
                phased[pl.ds(at * rows, rows), :] = (re * cosine + im * sine).astype(BF)
                phased[pl.ds((2 + at) * rows, rows), :] = (im * cosine - re * sine).astype(BF)

        q_re = dot_lines(phased[...], mat[0, 0])
        q_im = dot_lines(phased[...], mat[1, 0])
        n = 2 * rows
        new_re = (q_re[:n] - q_im[n:]).astype(BF)
        new_im = (q_re[n:] + q_im[:n]).astype(BF)
        for at, outs in enumerate(((m00, m10), (m01, m11))):

            @pl.when(b == at)
            def _(outs=outs):
                for w, out in enumerate(outs):
                    out[0] = new_re[w * rows : (w + 1) * rows]
                    out[1] = new_im[w * rows : (w + 1) * rows]

    message = ((2, rows, half), BF, (2, rows, half), lambda b, ids: (0, 0, 0))
    field = spec((2, 1, rows, cols), lambda b, ids: (0, ids[4] ^ turn, 0, 0))
    return call(
        body,
        (2,),
        [
            field,
            field,
            spec((2, 1, half, cols), lambda b, ids: (0, ids[4] ^ turn, ids[5] ^ b, 0)),
            spec((1, rows, cols), lambda b, ids: (0, 0, 0)),
            SMEM,
        ],
        [message] * 4,
        [pltpu.VMEM((4 * rows, cols), BF)],
        (ids, source, receiver, matrix, lens, omegas),
        2 * 4 * rows * cols * cols * 2,
        60 << 20,
    )


def trig(ids, stack, omega, by_rows):
    _, quarter, half = stack.shape
    slices = stack.shape[0] // 2
    rows, cols = (quarter, 2 * half) if by_rows else (2 * quarter, half)

    def body(ids, pieces, om, sine_ref, cosine_ref):
        s = pl.program_id(0)
        for side in range(2):
            at = ((ids[1] ^ side) * 2 + (ids[3] ^ (s % 2))) * 4 + (ids[2] ^ (s // 2))
            sine, cosine = sin_cos(pieces[at] * (om[0] * (TWO_OVER_PI / LENS_GAIN)))
            if by_rows:
                to = (slice(None), pl.ds(side * half, half))
            else:
                to = (pl.ds(side * quarter, quarter), slice(None))
            sine_ref[to] = sine
            cosine_ref[to] = cosine

    out = ((slices * rows, cols), F32, (rows, cols), lambda s, ids: (s, 0))
    return call(
        body,
        (slices,),
        [spec(stack.shape, lambda s, ids: (0, 0, 0)), SMEM],
        [out, out],
        [],
        (ids, stack, omega),
        1 << 26,
    )


def rotated(re, im, sine, cosine):
    return (re * cosine + im * sine).astype(BF), (im * cosine - re * sine).astype(BF)


def column_solve(ids, messages, matrix, waves):
    _, rows, half = messages[0].shape
    n = matrix.shape[-1]
    slices = n // rows
    tile = 2 * rows
    tiles = n // tile
    quarter = rows // 2
    per = tile // quarter
    blocked = matrix.reshape(2, slices, 2, quarter, n)

    def body(ids, *refs):
        (m0, m1, m2, m3, m4, m5, m6, m7, mat, mat_half, sine_ref, cosine_ref,
         keep, send, phased, out, field, sems) = refs
        i = pl.program_id(0)
        t = ids[4] * 2 + ids[3]

        @pl.when(i == 0)
        def _():
            copies = []
            for at, m in enumerate((m0, m1, m2, m3, m4, m5, m6, m7)):
                a, b = at // 2, at % 2
                place = (ids[0] ^ b) * 4 + (t ^ a)
                for part in range(2):
                    copies.append(
                        pltpu.make_async_copy(
                            m.at[part],
                            field.at[part, pl.ds(pl.multiple_of(place * rows, rows), rows)],
                            sems.at[at, part],
                        )
                    )
            for copy in copies:
                copy.start()
            for copy in copies:
                copy.wait()

        @pl.when(i < tiles)
        def _():
            left = mat[...].reshape(2 * tile, n)
            q_re = dot_rows(left, field[0])
            q_im = dot_rows(left, field[1])
            new_re = q_re[:tile] - q_im[tile:]
            new_im = q_im[:tile] + q_re[tile:]
            first = ids[3] == 0
            for part, new in enumerate((new_re, new_im)):
                even, odd = new[:rows].astype(BF), new[rows:].astype(BF)
                keep[part, i] = jnp.where(first, even, odd)
                send[part, i] = jnp.where(first, odd, even)
            re, im = rotated(new_re, new_im, sine_ref[...], cosine_ref[...])
            to = pl.ds(pl.multiple_of(i * tile, tile), tile)
            phased[0, to] = re
            phased[1, to] = im

        @pl.when(i >= tiles)
        def _():
            left = mat_half[...].reshape(2 * tile, n)
            q_re = dot_rows(left, phased[0])
            q_im = dot_rows(left, phased[1])
            to = pl.ds(pl.multiple_of((i - tiles) * tile, tile), tile)
            out[0, to] = (q_re[:tile] - q_im[tile:]).astype(BF)
            out[1, to] = (q_im[:tile] + q_re[tile:]).astype(BF)

    flat = lambda rank: (lambda i, ids: (0,) * rank)
    part_shape = (2, tiles, rows, half)
    return call(
        body,
        (tiles + tiles // 2,),
        [ANY] * 8
        + [
            spec((2, tile, n), lambda i, ids: (0, jnp.minimum(i, tiles - 1), 0)),
            spec(
                (2, per, 1, quarter, n),
                lambda i, ids: (0, jnp.maximum(i - tiles, 0), 1 - ids[0], 0, 0),
            ),
            spec((tile, half), lambda i, ids: (jnp.minimum(i, tiles - 1), 0)),
            spec((tile, half), lambda i, ids: (jnp.minimum(i, tiles - 1), 0)),
        ],
        [
            (part_shape, BF, part_shape, flat(4)),
            (part_shape, BF, part_shape, flat(4)),
            ((2, n, half), BF, (2, n, half), flat(3)),
            ((2, n // 2, half), BF, (2, n // 2, half), flat(3)),
        ],
        [pltpu.VMEM((2, n, half), BF), pltpu.SemaphoreType.DMA((8, 2))],
        (ids, *messages, matrix, blocked, *waves),
        12 * n * n * half,
    )


def column_rest(ids, phased, matrix, rows):
    _, n, half = phased.shape
    slices = n // rows
    tile = 2 * rows
    quarter = rows // 2
    per = tile // quarter
    blocked = matrix.reshape(2, slices, 2, quarter, n)

    def body(ids, field, mat_half, out):
        left = mat_half[...].reshape(2 * tile, n)
        q_re = dot_rows(left, field[0])
        q_im = dot_rows(left, field[1])
        out[0] = (q_re[:tile] - q_im[tile:]).astype(BF)
        out[1] = (q_im[:tile] + q_re[tile:]).astype(BF)

    return call(
        body,
        (slices * quarter // tile,),
        [
            spec((2, n, half), lambda i, ids: (0, 0, 0)),
            spec((2, per, 1, quarter, n), lambda i, ids: (0, i, ids[0], 0, 0)),
        ],
        [((2, n // 2, half), BF, (2, tile, half), lambda i, ids: (0, i, 0))],
        [],
        (ids, phased, blocked),
        4 * n * n * half,
    )[0]


def row_solve(ids, own, received, matrix, waves, rows):
    _, lines, half = own.shape
    n = matrix.shape[-1]
    slices = n // rows
    quarter = rows // 2
    tile = 2 * rows
    tiles = n // tile

    def body(ids, own_ref, rec_ref, mat, mat_half, sine_ref, cosine_ref, keep, send, phased, out, field):
        i = pl.program_id(0)

        @pl.when(i == 0)
        def _():
            for at, ref in enumerate((own_ref, rec_ref)):
                to = pl.ds(pl.multiple_of((ids[0] ^ at) * half, half), half)
                field[pl.ds(0, lines), to] = ref[0]
                field[pl.ds(lines, lines), to] = ref[1]

        @pl.when(i < tiles)
        def _():
            q_re = dot_lines(field[...], mat[0])
            q_im = dot_lines(field[...], mat[1])
            new_re = q_re[:lines] - q_im[lines:]
            new_im = q_re[lines:] + q_im[:lines]
            cols = pl.ds(pl.multiple_of(i * tile, tile), tile)
            first = ids[3] == 0
            re, im = rotated(new_re, new_im, sine_ref[...], cosine_ref[...])
            phased[0, :, cols] = re
            phased[1, :, cols] = im
            for part, new in enumerate((new_re, new_im)):
                for z in range(slices // 2):
                    lo = 2 * z * quarter
                    even = new[lo : lo + quarter].astype(BF)
                    odd = new[lo + quarter : lo + 2 * quarter].astype(BF)
                    keep[part, z, :, cols] = jnp.where(first, even, odd)
                    send[part, z, :, cols] = jnp.where(first, odd, even)

        @pl.when(i >= tiles)
        def _():
            left = phased[...].reshape(2 * lines, n)
            q_re = dot_lines(left, mat_half[0])
            q_im = dot_lines(left, mat_half[1])
            cols = pl.ds(pl.multiple_of((i - tiles) * tile, tile), tile)
            out[0, :, cols] = (q_re[:lines] - q_im[lines:]).astype(BF)
            out[1, :, cols] = (q_re[lines:] + q_im[:lines]).astype(BF)

    flat = lambda rank: (lambda i, ids: (0,) * rank)
    part_shape = (2, slices // 2, quarter, n)
    per_half = half // tile
    return call(
        body,
        (tiles + per_half,),
        [
            spec(own.shape, flat(3)),
            spec(own.shape, flat(3)),
            spec((2, tile, n), lambda i, ids: (0, jnp.minimum(i, tiles - 1), 0)),
            spec(
                (2, tile, n),
                lambda i, ids: (0, (1 - ids[0]) * per_half + jnp.maximum(i - tiles, 0), 0),
            ),
            spec((lines, tile), lambda i, ids: (0, jnp.minimum(i, tiles - 1))),
            spec((lines, tile), lambda i, ids: (0, jnp.minimum(i, tiles - 1))),
        ],
        [
            (part_shape, BF, part_shape, flat(4)),
            (part_shape, BF, part_shape, flat(4)),
            ((2, lines, n), BF, (2, lines, n), flat(3)),
            ((2, lines, half), BF, (2, lines, half), flat(3)),
        ],
        [pltpu.VMEM((2 * lines, n), BF)],
        (ids, own, received, matrix, matrix, *waves),
        12 * n * n * half,
    )


def row_rest(ids, phased, matrix, rows):
    _, lines, n = phased.shape
    half = n // 2
    tile = 2 * rows
    per_half = half // tile

    def body(ids, field, mat, out):
        left = field[...].reshape(2 * lines, n)
        q_re = dot_lines(left, mat[0])
        q_im = dot_lines(left, mat[1])
        out[0] = (q_re[:lines] - q_im[lines:]).astype(BF)
        out[1] = (q_re[lines:] + q_im[:lines]).astype(BF)

    return call(
        body,
        (per_half,),
        [
            spec(phased.shape, lambda i, ids: (0, 0, 0)),
            spec((2, tile, n), lambda i, ids: (0, ids[0] * per_half + i, 0)),
        ],
        [((2, lines, half), BF, (2, lines, tile), lambda i, ids: (0, 0, i))],
        [],
        (ids, phased, matrix),
        4 * n * n * half,
    )[0]


def last_solve(ids, turn, own, received, matrix, rows):
    _, _, half = own.shape
    n = matrix.shape[-1]
    slices = n // rows
    quarter = rows // 2
    tile = 2 * rows

    def body(ids, own_ref, rec_ref, mat, m00, m01, m10, m11, field):
        b = pl.program_id(0)

        @pl.when(b == 0)
        def _():
            for at, ref in enumerate((own_ref, rec_ref)):
                side = (ids[0] ^ at) * quarter
                for part in range(2):
                    for s in range(slices):
                        to = pl.ds(pl.multiple_of(s * rows + side, quarter), quarter)
                        field[part, to] = ref[part, pl.ds(s * quarter, quarter)]

        left = mat[...].reshape(2 * tile, n)
        q_re = dot_rows(left, field[0])
        q_im = dot_rows(left, field[1])
        new_re = (q_re[:tile] - q_im[tile:]).astype(BF)
        new_im = q_im[:tile] + q_re[tile:]
        first = ids[3] == 0
        new_im = jnp.where(first, new_im, -new_im).astype(BF)
        for at, (near, far) in enumerate(((m00, m10), (m01, m11))):

            @pl.when(b == at)
            def _(near=near, far=far):
                for part, new in enumerate((new_re, new_im)):
                    near[part] = jnp.where(first, new[:rows], new[rows:])
                    far[part] = jnp.where(first, new[rows:], new[:rows])

    message = ((2, rows, half), BF, (2, rows, half), lambda b, ids: (0, 0, 0))
    return call(
        body,
        (2,),
        [
            spec(own.shape, lambda b, ids: (0, 0, 0)),
            spec(own.shape, lambda b, ids: (0, 0, 0)),
            spec((2, tile, n), lambda b, ids: (0, (ids[0] ^ b) * 2 + (ids[4] ^ turn), 0)),
        ],
        [message] * 4,
        [pltpu.VMEM((2, n, half), BF)],
        (ids, own, received, matrix),
        4 * n * n * half,
    )


def arrive(ids, messages, image_weights, freqs):
    _, rows, half = messages[0].shape

    def body(ids, *refs):
        ms, (wt, src, rec, grad, held, sems) = refs[:8], refs[8:]
        copies = [
            pltpu.make_async_copy(m, held.at[at], sems.at[at]) for at, m in enumerate(ms)
        ]
        for copy in copies:
            copy.start()
        for copy in copies:
            copy.wait()
        for side in range(2):
            total = None
            for j in range(freqs):
                a_hi = ids[4] ^ j
                b = ids[5] ^ side
                s_at = (a_hi * 2 + ids[3]) * 2 + b
                r_at = (a_hi * 2 + (1 - ids[3])) * 2 + b
                s, r = held[s_at], held[r_at]
                cols = pl.ds(side * half, half)
                src[:, j, :, cols] = s
                rec[:, j, :, cols] = r
                s, r = s.astype(F32), r.astype(F32)
                term = wt[j] * (s[0] * r[0] + s[1] * r[1])
                total = term if total is None else total + term
            grad[:, pl.ds(side * half, half)] = total.astype(BF)

    flat = lambda rank: (lambda i, ids: (0,) * rank)
    full = (2, freqs, rows, 2 * half)
    return call(
        body,
        (1,),
        [ANY] * 8 + [SMEM],
        [
            (full, BF, full, flat(4)),
            (full, BF, full, flat(4)),
            ((rows, 2 * half), BF, (rows, 2 * half), flat(2)),
        ],
        [pltpu.VMEM((8, 2, rows, half), BF), pltpu.SemaphoreType.DMA((8,))],
        (ids, *messages, image_weights),
        1 << 22,
    )


def image_terms(ids, keep, other, weight, by_rows):
    _, lines, rows, cols = keep.shape
    high, wide = (rows, cols // 2) if by_rows else (rows // 2, cols)

    def body(ids, k, o, wt, stay, away):
        first = ids[1] == 0
        re = k[0, 0].astype(F32) * o[0, 0].astype(F32)
        term = wt[0] * (re - k[1, 0].astype(F32) * o[1, 0].astype(F32))
        lo, hi = (term[:, :wide], term[:, wide:]) if by_rows else (term[:high], term[high:])
        stay[0] = jnp.where(first, lo, hi)
        away[0] = jnp.where(first, hi, lo).astype(BF)

    block = spec((2, 1, rows, cols), lambda i, ids: (0, i, 0, 0))
    shape, piece = (lines, high, wide), (1, high, wide)
    index = lambda i, ids: (i, 0, 0)
    return call(
        body,
        (lines,),
        [block, block, SMEM],
        [(shape, F32, piece, index), (shape, BF, piece, index)],
        [],
        (ids, keep, other, weight),
        1 << 22,
    )


def flip(size, bit):
    return [(i, i ^ bit) for i in range(size)]


def scatter_rounds(groups, space, back):
    rounds = []
    for a in range(4):
        for b in range(2):
            perm = []
            for x in range(groups // 2):
                for c in range(2):
                    for s in range(space):
                        home = (2 * x + c) * space + s
                        away = (2 * x + ((s // 4) ^ b)) * space + 4 * c + ((s % 4) ^ a)
                        perm.append((away, home) if back else (home, away))
            rounds.append(perm)
    return rounds


def plane_per_chip(source, receiver, matrix, lens, omegas, image_weights):
    groups, space = lax.axis_size("freq"), lax.axis_size("space")
    both = ("freq", "space")
    _, freqs, rows, cols = source.shape
    half, quarter = cols // 2, rows // 2
    group, s = lax.axis_index("freq"), lax.axis_index("space")
    core, x, z, y = group % 2, group // 2, s // 2, s % 2
    ids = jnp.stack([core, x, z, y, z % 2, z // 2]).astype(jnp.int32)
    swap = flip(groups, 1)

    going, coming = scatter_rounds(groups, space, False), scatter_rounds(groups, space, True)

    def send(outputs, turn, rounds):
        return [lax.ppermute(m, both, rounds[4 * turn + at]) for at, m in enumerate(outputs)]

    corners = ((1, x * quarter, core * half), (2, core * quarter, x * half))
    piece = jnp.concatenate(
        [lax.dynamic_slice(lens, corner, (1, quarter, half)) for corner in corners]
    )
    piece = (piece * LENS_GAIN).astype(jnp.float16)
    line = [piece] + [lax.ppermute(piece, "space", flip(space, 2 * k)) for k in (1, 2, 3)]
    line = jnp.stack(line, axis=1)
    across_y = lax.ppermute(line, "space", flip(space, 1))
    planes = [jnp.concatenate([line[d], across_y[d]]) for d in range(2)]
    across_x = [lax.ppermute(planes[d], "freq", flip(groups, 2)) for d in range(2)]

    solved = home_solve(ids, 0, source, receiver, matrix, lens, omegas)
    messages = send(solved, 0, going)
    solved = home_solve(ids, 1, source, receiver, matrix, lens, omegas)
    messages += send(solved, 1, going)

    mine = core == z // 2
    scalars = jnp.stack([omegas, image_weights])
    other = lax.ppermute(scalars, "freq", swap)
    omega, weight = jnp.where(mine, scalars, other)[:, z % 2]
    omega, weight = omega.reshape(1), weight.reshape(1)
    held = lax.dynamic_slice(matrix, (0, z % 2, 0, 0), (2, 1, cols, cols))[:, 0]
    theirs = lax.ppermute(held, "freq", swap)
    line_matrix = jnp.where(mine, held, theirs)

    waves = []
    for d in range(2):
        stack = jnp.concatenate([planes[d], across_x[d]]).astype(F32)
        waves.append(trig(ids, stack, omega, d == 1))

    keep0, send0, phased, sent = column_solve(ids, messages, line_matrix, waves[0])
    came = lax.ppermute(sent, "freq", swap)
    partner0 = lax.ppermute(send0, "space", flip(space, 1))
    own = column_rest(ids, phased, line_matrix, rows)
    keep1, send1, phased, sent = row_solve(ids, own, came, line_matrix, waves[1], rows)
    came = lax.ppermute(sent, "freq", swap)
    partner1 = lax.ppermute(send1, "space", flip(space, 1))
    own = row_rest(ids, phased, line_matrix, rows)

    solved = last_solve(ids, 0, own, came, line_matrix, rows)
    finals = send(solved, 0, coming)
    solved = last_solve(ids, 1, own, came, line_matrix, rows)
    finals += send(solved, 1, coming)

    pieces = []
    for depth, keep, partner in ((0, keep0, partner0), (1, keep1, partner1)):
        stay, away = image_terms(ids, keep, partner, weight, depth == 1)
        over_x = stay + lax.ppermute(away, "freq", flip(groups, 2)).astype(F32)

        def slab(at):
            return lax.dynamic_index_in_dim(over_x, at, 0, keepdims=False)

        total = slab(z)
        for k in (1, 2, 3):
            part = lax.ppermute(slab(z ^ k).astype(BF), "space", flip(space, 2 * k))
            total = total + part.astype(F32)
        pieces.append(total.astype(BF))
    piece = jnp.stack(pieces)
    pair = jnp.stack([piece, lax.ppermute(piece, "freq", swap)])
    quad = jnp.stack([pair, lax.ppermute(pair, "freq", flip(groups, 2))])

    def at_of(px, pc, depth):
        return lax.dynamic_slice(
            quad, (x ^ px, core ^ pc, depth, 0, 0), (1, 1, 1, quarter, half)
        )[0, 0, 0].astype(F32)

    grad0 = jnp.block([[at_of(0, 0, 0), at_of(0, 1, 0)], [at_of(1, 0, 0), at_of(1, 1, 0)]])
    grad1 = jnp.block([[at_of(0, 0, 1), at_of(1, 0, 1)], [at_of(0, 1, 1), at_of(1, 1, 1)]])

    source_out, receiver_out, term2 = arrive(ids, finals, image_weights, freqs)
    chip = term2.astype(F32) + lax.ppermute(term2, "freq", swap).astype(F32)
    grad2 = chip + lax.ppermute(chip.astype(BF), "freq", flip(groups, 2)).astype(F32)
    return source_out, receiver_out, jnp.stack([grad0, grad1, grad2])


def to_blocks(matrix, pieces):
    leading = matrix.shape[:-2]
    local_rows = matrix.shape[-2]
    columns = matrix.shape[-1] // pieces
    arranged = matrix.reshape(leading + (local_rows, pieces, columns))
    arranged = jnp.moveaxis(arranged, -2, -3)
    return arranged.reshape(leading + (pieces, local_rows * columns))


def from_blocks(blocked, local_rows):
    leading = blocked.shape[:-2]
    pieces = blocked.shape[-2]
    columns = blocked.shape[-1] // local_rows
    arranged = blocked.reshape(leading + (pieces, local_rows, columns))
    arranged = jnp.moveaxis(arranged, -1, -3)
    return arranged.reshape(leading + (columns, pieces * local_rows))


def rotate(fields, phase_angle):
    cosine = jnp.cos(phase_angle)
    sine_part = jnp.sin(phase_angle)
    flip_sign = jnp.array([1.0, -1.0], jnp.float32).reshape(2, 1, 1, 1)
    real_part = fields[:, 0]
    imag_part = fields[:, 1]
    return jnp.stack(
        [
            real_part * cosine + flip_sign * imag_part * sine_part,
            imag_part * cosine - flip_sign * real_part * sine_part,
        ],
        axis=1,
    )


def line_solve(line_inverse, fields):
    flip_sign = jnp.array([1.0, -1.0], jnp.float32).reshape(2, 1, 1, 1)
    prod_real = jnp.einsum(
        "fij,wpfrj->wpfri", line_inverse[0], fields, preferred_element_type=jnp.float32
    )
    prod_imag = jnp.einsum(
        "fij,wpfrj->wpfri", line_inverse[1], fields, preferred_element_type=jnp.float32
    )
    new_real = prod_real[:, 0] - flip_sign * prod_imag[:, 1]
    new_imag = prod_real[:, 1] + flip_sign * prod_imag[:, 0]
    return jnp.stack([new_real, new_imag], axis=1)


def march_step(line_inverse, phased, local_rows):
    pieces = lax.axis_size("space")
    across = line_solve(line_inverse, phased).astype(jnp.bfloat16)
    received = lax.all_to_all(
        to_blocks(across, pieces), "space", split_axis=3, concat_axis=3, tiled=True
    )
    return line_solve(line_inverse, from_blocks(received, local_rows))


def image_slice(fields, image_weights):
    image_term = fields[0, 0] * fields[1, 0] + fields[0, 1] * fields[1, 1]
    return jnp.sum(image_weights[:, None, None] * image_term, axis=0)


def reduce_slice(image_term):
    return lax.psum(image_term.astype(jnp.bfloat16), "freq").astype(jnp.float32)


def finish_sums(slices):
    stacked = jnp.stack(slices)
    return stacked


def general(source_field, receiver_field, line_inverse, lens_delay, omegas, image_weights):
    pieces = lax.axis_size("space")
    local_rows = lens_delay.shape[1]
    depth_count = lens_delay.shape[0]
    wavefields = jnp.stack([source_field, receiver_field]).astype(jnp.float32)
    slices = []
    lens_columns = from_blocks(
        lax.all_to_all(
            to_blocks(lens_delay, pieces), "space", split_axis=1, concat_axis=1, tiled=True
        ),
        local_rows,
    )
    phased = rotate(wavefields, omegas[:, None, None] * lens_delay[0][None]).astype(jnp.bfloat16)
    solved = march_step(line_inverse, phased, local_rows)
    slices.append(reduce_slice(image_slice(solved, image_weights)))
    for depth_step in range(1, depth_count):
        phase_angle = omegas[:, None, None] * lens_columns[depth_step][None]
        phased_columns = rotate(solved, phase_angle).astype(jnp.bfloat16)
        received = lax.all_to_all(
            to_blocks(phased_columns, pieces), "space", split_axis=3, concat_axis=3, tiled=True
        )
        solved = march_step(line_inverse, from_blocks(received, local_rows), local_rows)
        slices.append(reduce_slice(image_slice(solved, image_weights)))
    final_blocks = lax.all_to_all(
        to_blocks(solved.astype(jnp.bfloat16), pieces),
        "space",
        split_axis=3,
        concat_axis=3,
        tiled=True,
    )
    final_fields = from_blocks(final_blocks, local_rows)
    gradient_columns = finish_sums(slices)
    gradient = from_blocks(
        lax.all_to_all(
            to_blocks(gradient_columns, pieces).astype(jnp.bfloat16),
            "space",
            split_axis=1,
            concat_axis=1,
            tiled=True,
        ).astype(jnp.float32),
        local_rows,
    )
    return (final_fields[0], final_fields[1], gradient)


def on_device(source_field, receiver_field, line_inverse, lens_delay, omegas, image_weights):
    args = (source_field, receiver_field, line_inverse, lens_delay, omegas, image_weights)
    groups, space = lax.axis_size("freq"), lax.axis_size("space")
    freqs, depths = omegas.shape[0], lens_delay.shape[0]
    fits = space == 2 * 2 * freqs and freqs == 2 and groups % 4 == 0 and depths == 3
    if not fits:
        return general(*args)
    return plane_per_chip(*args)


def solution(mesh):
    placed = (
        P(None, "freq", "space", None),
        P(None, "freq", "space", None),
        P(None, "freq", None, None),
        P(None, "space", None),
        P("freq"),
        P("freq"),
    )
    return jax.shard_map(
        on_device,
        mesh=mesh,
        in_specs=placed,
        out_specs=(
            P(None, "freq", "space", None),
            P(None, "freq", "space", None),
            P(None, "space", None),
        ),
        check_vma=False,
    )
```

```python
import jax
import jax.numpy as jnp
from jax import lax
from jax.experimental import pallas as pl
from jax.experimental.pallas import tpu as pltpu
from jax.sharding import PartitionSpec as P


BF = jnp.bfloat16
F32 = jnp.float32
CHUNKS = 1
TILES = 2
GRANT = 16
TWO_OVER_PI = 0.63661977236758134
LENS_GAIN = 1.66
ANY = pl.BlockSpec(memory_space=pl.ANY)
SMEM = pl.BlockSpec(memory_space=pltpu.SMEM)


def sin_cos(quarter_turns):
    whole = jnp.round(quarter_turns)
    r = quarter_turns - whole
    q = r * r
    s = -0.00460174 * q + 0.07968794
    s = s * q - 0.64596367
    s = (s * q + 1.57079632) * r
    c = 0.00091925 * q - 0.02086341
    c = c * q + 0.25366950
    c = c * q - 1.23370055
    c = c * q + 1.0
    k = whole.astype(jnp.int32)
    odd = (k & 1) == 1
    sine = jnp.where(odd, c, s)
    cosine = jnp.where(odd, s, c)
    sine = jnp.where((k & 2) == 2, -sine, sine)
    cosine = jnp.where(((k + 1) & 2) == 2, -cosine, cosine)
    return sine, cosine


def dot_rows(a, b):
    return lax.dot_general(a, b, (((1,), (0,)), ((), ())), preferred_element_type=F32)


def dot_lines(a, b):
    return lax.dot_general(a, b, (((1,), (1,)), ((), ())), preferred_element_type=F32)


def spec(block, index):
    return pl.BlockSpec(block, index)


def call(body, grid, ins, outs, scratch, operands, cost, limit=28 << 20):
    return pl.pallas_call(
        body,
        out_shape=[jax.ShapeDtypeStruct(s, d) for s, d, _, _ in outs],
        grid_spec=pltpu.PrefetchScalarGridSpec(
            num_scalar_prefetch=1,
            grid=grid,
            in_specs=ins,
            out_specs=[pl.BlockSpec(b, i) for _, _, b, i in outs],
            scratch_shapes=scratch,
        ),
        compiler_params=pltpu.CompilerParams(vmem_limit_bytes=limit),
        cost_estimate=pl.CostEstimate(flops=cost, bytes_accessed=8 << 20, transcendentals=0),
    )(*operands)


VMEM = pl.BlockSpec(memory_space=pltpu.VMEM)


def solid(body, outs, scratch, operands, cost, limit, ins=None):
    return pl.pallas_call(
        body,
        out_shape=[jax.ShapeDtypeStruct(s, d) for s, d in outs],
        in_specs=[SMEM] + (ins or [VMEM] * (len(operands) - 1)),
        out_specs=[VMEM] * len(outs),
        scratch_shapes=scratch,
        compiler_params=pltpu.CompilerParams(vmem_limit_bytes=limit << 20),
        cost_estimate=pl.CostEstimate(flops=cost, bytes_accessed=8 << 20, transcendentals=0),
    )(*operands)


def home_solve(ids, turn, source, receiver, matrix, lens, omegas):
    _, _, rows, cols = source.shape
    half = cols // 2

    def body(ids, src, rec, mat, len_ref, om, m00, m01, m10, m11, phased):
        b = pl.program_id(0)
        y = ids[3]
        j = ids[4] ^ turn

        @pl.when(b == 0)
        def _():
            sine, cosine = sin_cos(len_ref[0] * (om[j] * TWO_OVER_PI))
            sr = src[0, 0].astype(F32)
            si = src[1, 0].astype(F32)
            rr = rec[0, 0].astype(F32)
            ri = -rec[1, 0].astype(F32)
            first = y == 0
            for at, (re, im) in enumerate(
                (
                    (jnp.where(first, sr, rr), jnp.where(first, si, ri)),
                    (jnp.where(first, rr, sr), jnp.where(first, ri, si)),
                )
            ):
                phased[pl.ds(at * rows, rows), :] = (re * cosine + im * sine).astype(BF)
                phased[pl.ds((2 + at) * rows, rows), :] = (im * cosine - re * sine).astype(BF)

        q_re = dot_lines(phased[...], mat[0, 0])
        q_im = dot_lines(phased[...], mat[1, 0])
        n = 2 * rows
        new_re = (q_re[:n] - q_im[n:]).astype(BF)
        new_im = (q_re[n:] + q_im[:n]).astype(BF)
        for at, outs in enumerate(((m00, m10), (m01, m11))):

            @pl.when(b == at)
            def _(outs=outs):
                for w, out in enumerate(outs):
                    out[0] = new_re[w * rows : (w + 1) * rows]
                    out[1] = new_im[w * rows : (w + 1) * rows]

    message = ((2, rows, half), BF, (2, rows, half), lambda b, ids: (0, 0, 0))
    field = spec((2, 1, rows, cols), lambda b, ids: (0, ids[4] ^ turn, 0, 0))
    return call(
        body,
        (2,),
        [
            field,
            field,
            spec((2, 1, half, cols), lambda b, ids: (0, ids[4] ^ turn, ids[5] ^ b, 0)),
            spec((1, rows, cols), lambda b, ids: (0, 0, 0)),
            SMEM,
        ],
        [message] * 4,
        [pltpu.VMEM((4 * rows, cols), BF)],
        (ids, source, receiver, matrix, lens, omegas),
        2 * 4 * rows * cols * cols * 2,
        60 << 20,
    )


def trig(ids, stack, omega, by_rows):
    _, quarter, half = stack.shape
    slices = stack.shape[0] // 2
    rows, cols = (quarter, 2 * half) if by_rows else (2 * quarter, half)

    def body(ids, pieces, om, sine_ref, cosine_ref):
        s = pl.program_id(0)
        for side in range(2):
            x_at, y_at = ids[1] ^ side, ids[3] ^ (s % 2)
            at = (x_at * 2 + y_at) * 4 + (ids[2] ^ (s // 2))
            sine, cosine = sin_cos(pieces[at] * (om[0] * (TWO_OVER_PI / LENS_GAIN)))
            if by_rows:
                to = (slice(None), pl.ds(side * half, half))
            else:
                to = (pl.ds(side * quarter, quarter), slice(None))
            sine_ref[to] = sine
            cosine_ref[to] = cosine

    out = ((slices * rows, cols), F32, (rows, cols), lambda s, ids: (s, 0))
    return call(
        body,
        (slices,),
        [spec(stack.shape, lambda s, ids: (0, 0, 0)), SMEM],
        [out, out],
        [],
        (ids, stack, omega),
        1 << 26,
        12 << 20,
    )


def rotated(re, im, sine, cosine):
    return (re * cosine + im * sine).astype(BF), (im * cosine - re * sine).astype(BF)


def column_solve(ids, messages, matrix, waves):
    _, rows, half = messages[0].shape
    n = matrix.shape[-1]
    slices = n // rows
    tile = n // TILES
    chunk = half // CHUNKS
    quarter = rows // 2
    blocked = matrix.reshape(2, slices, 2, quarter, n)

    def body(ids, *refs):
        ms, (mat, sine_ref, cosine_ref, keep, send, phased, out, field) = refs[:8], refs[8:]
        t = ids[4] * 2 + ids[3]
        for at, m in enumerate(ms):
            a, b = at // 2, at % 2
            place = (ids[0] ^ b) * 4 + (t ^ a)
            to = pl.ds(pl.multiple_of(place * rows, rows), rows)
            field[0, to] = m[0]
            field[1, to] = m[1]
        first = ids[3] == 0
        for i in range(TILES):
            per = tile // rows
            left = mat[:, i * per : (i + 1) * per].reshape(2 * tile, n)
            to = pl.ds(i * tile, tile)
            for c in range(CHUNKS):
                cols = pl.ds(c * chunk, chunk)
                q_re = dot_rows(left, field[0, :, cols])
                q_im = dot_rows(left, field[1, :, cols])
                new_re = q_re[:tile] - q_im[tile:]
                new_im = q_im[:tile] + q_re[tile:]
                re, im = rotated(new_re, new_im, sine_ref[to, cols], cosine_ref[to, cols])
                phased[0, to, cols] = re
                phased[1, to, cols] = im
                for part, new in enumerate((new_re, new_im)):
                    for line in range(per // 2):
                        lo = 2 * line * rows
                        even = new[lo : lo + rows].astype(BF)
                        odd = new[lo + rows : lo + 2 * rows].astype(BF)
                        z = i * (per // 2) + line
                        keep[part, z, :, cols] = jnp.where(first, even, odd)
                        send[part, z, :, cols] = jnp.where(first, odd, even)
        column_half(mat, 1 - ids[0], phased, out)

    part = ((2, slices // 2, rows, half), BF)
    return solid(
        body,
        [part, part, ((2, n, half), BF), ((2, n // 2, half), BF)],
        [pltpu.VMEM((2, n, half), BF)],
        (ids, *messages, blocked, *waves),
        12 * n * n * half,
        GRANT,
    )


def column_half(mat, side, field, out):
    _, _, _, _, n = mat.shape
    tile = n // 2
    half = field.shape[-1]
    chunk = half // CHUNKS
    left = mat[:, :, side].reshape(2 * tile, n)
    for c in range(CHUNKS):
        cols = pl.ds(c * chunk, chunk)
        q_re = dot_rows(left, field[0, :, cols])
        q_im = dot_rows(left, field[1, :, cols])
        out[0, :, cols] = (q_re[:tile] - q_im[tile:]).astype(BF)
        out[1, :, cols] = (q_im[:tile] + q_re[tile:]).astype(BF)


def column_rest(ids, phased, matrix, rows):
    _, n, half = phased.shape
    blocked = matrix.reshape(2, n // rows, 2, rows // 2, n)

    def body(ids, field, mat, out):
        column_half(mat, ids[0], field, out)

    return solid(
        body,
        [((2, n // 2, half), BF)],
        [],
        (ids, phased, blocked),
        4 * n * n * half,
        GRANT,
    )[0]


def row_solve(ids, own, received, matrix, waves, rows):
    _, lines, half = own.shape
    n = matrix.shape[-1]
    slices = n // rows
    quarter = rows // 2
    tile = n // TILES

    def body(ids, own_ref, rec_ref, mat, sine_ref, cosine_ref, keep, send, phased, out, field):
        for at, ref in enumerate((own_ref, rec_ref)):
            to = pl.ds(pl.multiple_of((ids[0] ^ at) * half, half), half)
            field[pl.ds(0, lines), to] = ref[0]
            field[pl.ds(lines, lines), to] = ref[1]
        first = ids[3] == 0
        for i in range(TILES * CHUNKS):
            cols = pl.ds(i * (tile // CHUNKS), tile // CHUNKS)
            q_re = dot_lines(field[...], mat[0, cols])
            q_im = dot_lines(field[...], mat[1, cols])
            new_re = q_re[:lines] - q_im[lines:]
            new_im = q_re[lines:] + q_im[:lines]
            re, im = rotated(new_re, new_im, sine_ref[:, cols], cosine_ref[:, cols])
            phased[0, :, cols] = re
            phased[1, :, cols] = im
            for part, new in enumerate((new_re, new_im)):
                for z in range(slices // 2):
                    lo = 2 * z * quarter
                    even = new[lo : lo + quarter].astype(BF)
                    odd = new[lo + quarter : lo + 2 * quarter].astype(BF)
                    keep[part, z, :, cols] = jnp.where(first, even, odd)
                    send[part, z, :, cols] = jnp.where(first, odd, even)
        row_half(mat, 1 - ids[0], phased, out)

    part = ((2, slices // 2, quarter, n), BF)
    return solid(
        body,
        [part, part, ((2, lines, n), BF), ((2, lines, half), BF)],
        [pltpu.VMEM((2 * lines, n), BF)],
        (ids, own, received, matrix, *waves),
        12 * n * n * half,
        GRANT,
    )


def row_half(mat, side, field, out):
    _, lines, n = field.shape
    half = n // 2
    chunk = half // CHUNKS
    left = field[...].reshape(2 * lines, n)
    for c in range(CHUNKS):
        at = pl.ds(pl.multiple_of(side * half + c * chunk, chunk), chunk)
        q_re = dot_lines(left, mat[0, at])
        q_im = dot_lines(left, mat[1, at])
        cols = pl.ds(c * chunk, chunk)
        out[0, :, cols] = (q_re[:lines] - q_im[lines:]).astype(BF)
        out[1, :, cols] = (q_re[lines:] + q_im[:lines]).astype(BF)


def row_rest(ids, phased, matrix):
    _, lines, n = phased.shape

    def body(ids, field, mat, out):
        row_half(mat, ids[0], field, out)

    return solid(
        body,
        [((2, lines, n // 2), BF)],
        [],
        (ids, phased, matrix),
        4 * n * n * (n // 2),
        GRANT,
    )[0]


def last_solve(ids, turn, own, received, matrix, rows):
    _, _, half = own.shape
    n = matrix.shape[-1]
    slices = n // rows
    quarter = rows // 2
    tile = 2 * rows

    def body(ids, own_ref, rec_ref, mat, m00, m01, m10, m11, field):
        for at, ref in enumerate((own_ref, rec_ref)):
            side = (ids[0] ^ at) * quarter
            for part in range(2):
                for s in range(slices):
                    to = pl.ds(pl.multiple_of(s * rows + side, quarter), quarter)
                    field[part, to] = ref[part, pl.ds(s * quarter, quarter)]
        first = ids[3] == 0
        for b, (near, far) in enumerate(((m00, m10), (m01, m11))):
            at = (ids[0] ^ b) * 2 + (ids[4] ^ turn)
            left = mat[:, pl.ds(pl.multiple_of(at * tile, tile), tile)].reshape(2 * tile, n)
            q_re = dot_rows(left, field[0])
            q_im = dot_rows(left, field[1])
            new_re = (q_re[:tile] - q_im[tile:]).astype(BF)
            new_im = q_im[:tile] + q_re[tile:]
            new_im = jnp.where(first, new_im, -new_im).astype(BF)
            for part, new in enumerate((new_re, new_im)):
                near[part] = jnp.where(first, new[:rows], new[rows:])
                far[part] = jnp.where(first, new[rows:], new[:rows])

    return solid(
        body,
        [((2, rows, half), BF)] * 4,
        [pltpu.VMEM((2, n, half), BF)],
        (ids, own, received, matrix),
        4 * n * n * half,
        GRANT,
    )


def last_term(ids, messages, image_weights):
    _, rows, half = messages[0].shape
    high = rows // 2

    def body(ids, *refs):
        ms, (wt, stay, away) = refs[:8], refs[8:]
        sides = []
        for b in range(2):
            total = None
            for turn in range(2):
                s, r = ms[4 * turn + b], ms[4 * turn + 2 + b]
                term = s[0].astype(F32) * r[0].astype(F32) + s[1].astype(F32) * r[1].astype(F32)
                term = wt[ids[4] ^ turn] * term
                total = term if total is None else total + term
            sides.append(total)
        left = ids[5] == 0
        for b in range(2):
            value = jnp.where(left, sides[b], sides[1 - b])
            lo, hi = value[:high], value[high:]
            first = ids[0] == 0
            cols = pl.ds(b * half, half)
            stay[:, cols] = jnp.where(first, lo, hi)
            away[:, cols] = jnp.where(first, hi, lo).astype(BF)

    shape = (high, 2 * half)
    index = lambda i, ids: (0, 0)
    return call(
        body,
        (1,),
        [spec((2, rows, half), lambda i, ids: (0, 0, 0))] * 8 + [SMEM],
        [(shape, F32, shape, index), (shape, BF, shape, index)],
        [],
        (ids, *messages, image_weights),
        1 << 22,
        14 << 20,
    )


def arrive(ids, messages, freqs):
    _, rows, half = messages[0].shape

    def body(ids, *refs):
        ms, (src, rec, held, sems) = refs[:8], refs[8:]
        copies = [
            pltpu.make_async_copy(m, held.at[at], sems.at[at]) for at, m in enumerate(ms)
        ]
        for copy in copies:
            copy.start()
        for copy in copies:
            copy.wait()
        for side in range(2):
            for j in range(freqs):
                a_hi = ids[4] ^ j
                b = ids[5] ^ side
                cols = pl.ds(side * half, half)
                src[:, j, :, cols] = held[(a_hi * 2 + ids[3]) * 2 + b]
                rec[:, j, :, cols] = held[(a_hi * 2 + (1 - ids[3])) * 2 + b]

    full = (2, freqs, rows, 2 * half)
    index = lambda i, ids: (0, 0, 0, 0)
    return call(
        body,
        (1,),
        [ANY] * 8,
        [(full, BF, full, index), (full, BF, full, index)],
        [pltpu.VMEM((8, 2, rows, half), BF), pltpu.SemaphoreType.DMA((8,))],
        (ids, *messages),
        1 << 22,
        12 << 20,
    )


def image_terms(ids, keep, other, weight, by_rows):
    _, lines, rows, cols = keep.shape
    high, wide = (rows, cols // 2) if by_rows else (rows // 2, cols)

    def body(ids, k, o, wt, stay, away):
        first = ids[1] == 0
        re = k[0, 0].astype(F32) * o[0, 0].astype(F32)
        term = wt[0] * (re - k[1, 0].astype(F32) * o[1, 0].astype(F32))
        lo, hi = (term[:, :wide], term[:, wide:]) if by_rows else (term[:high], term[high:])
        stay[0] = jnp.where(first, lo, hi)
        away[0] = jnp.where(first, hi, lo).astype(BF)

    block = spec((2, 1, rows, cols), lambda i, ids: (0, i, 0, 0))
    shape, piece = (lines, high, wide), (1, high, wide)
    index = lambda i, ids: (i, 0, 0)
    return call(
        body,
        (lines,),
        [block, block, SMEM],
        [(shape, F32, piece, index), (shape, BF, piece, index)],
        [],
        (ids, keep, other, weight),
        1 << 22,
        8 << 20,
    )


def gradient_rows(ids, quad, mine, theirs):
    quarter, half = quad.shape[-2:]
    rows, cols = 2 * quarter, 2 * half

    def body(ids, quad_ref, mine_ref, theirs_ref, out):
        for a in range(2):
            for b in range(2):
                to = (pl.ds(a * quarter, quarter), pl.ds(b * half, half))
                out[(0, *to)] = quad_ref[ids[1] ^ a, ids[0] ^ b, 0].astype(F32)
                out[(1, *to)] = quad_ref[ids[1] ^ b, ids[0] ^ a, 1].astype(F32)
        first = ids[0] == 0
        own, other = mine_ref[...].astype(F32), theirs_ref[...].astype(F32)
        out[2, pl.ds(0, quarter)] = jnp.where(first, own, other)
        out[2, pl.ds(quarter, quarter)] = jnp.where(first, other, own)

    flat = lambda rank: (lambda i, ids: (0,) * rank)
    full = (3, rows, cols)
    return call(
        body,
        (1,),
        [spec(quad.shape, flat(5)), spec(mine.shape, flat(2)), spec(mine.shape, flat(2))],
        [(full, F32, full, flat(3))],
        [],
        (ids, quad, mine, theirs),
        1 << 20,
        8 << 20,
    )[0]


def flip(size, bit):
    return [(i, i ^ bit) for i in range(size)]


def scatter_rounds(groups, space, back):
    rounds = []
    for a in range(4):
        for b in range(2):
            perm = []
            for x in range(groups // 2):
                for c in range(2):
                    for s in range(space):
                        home = (2 * x + c) * space + s
                        away = (2 * x + ((s // 4) ^ b)) * space + 4 * c + ((s % 4) ^ a)
                        perm.append((away, home) if back else (home, away))
            rounds.append(perm)
    return rounds


def plane_per_chip(source, receiver, matrix, lens, omegas, image_weights):
    groups, space = lax.axis_size("freq"), lax.axis_size("space")
    both = ("freq", "space")
    _, freqs, rows, cols = source.shape
    half, quarter = cols // 2, rows // 2
    group, s = lax.axis_index("freq"), lax.axis_index("space")
    core, x, z, y = group % 2, group // 2, s // 2, s % 2
    ids = jnp.stack([core, x, z, y, z % 2, z // 2]).astype(jnp.int32)
    swap = flip(groups, 1)

    going, coming = scatter_rounds(groups, space, False), scatter_rounds(groups, space, True)

    def send(outputs, turn, rounds):
        return [lax.ppermute(m, both, rounds[4 * turn + at]) for at, m in enumerate(outputs)]

    corners = ((1, x * quarter, core * half), (2, core * quarter, x * half))
    piece = jnp.concatenate(
        [lax.dynamic_slice(lens, corner, (1, quarter, half)) for corner in corners]
    )
    piece = (piece * LENS_GAIN).astype(jnp.float16)
    line = [piece] + [lax.ppermute(piece, "space", flip(space, 2 * k)) for k in (1, 2, 3)]
    line = jnp.stack(line, axis=1)
    other_line = lax.ppermute(line, "space", flip(space, 1))
    planes = [jnp.concatenate([line[d], other_line[d]]) for d in range(2)]
    stacks = [
        jnp.concatenate([planes[d], lax.ppermute(planes[d], "freq", flip(groups, 2))])
        for d in range(2)
    ]

    solved = home_solve(ids, 0, source, receiver, matrix, lens, omegas)
    messages = send(solved, 0, going)
    solved = home_solve(ids, 1, source, receiver, matrix, lens, omegas)
    messages += send(solved, 1, going)

    mine = core == z // 2
    scalars = jnp.stack([omegas, image_weights])
    other = lax.ppermute(scalars, "freq", swap)
    omega, weight = jnp.where(mine, scalars, other)[:, z % 2]
    omega, weight = omega.reshape(1), weight.reshape(1)
    held = lax.dynamic_slice(matrix, (0, z % 2, 0, 0), (2, 1, cols, cols))[:, 0]
    theirs = lax.ppermute(held, "freq", swap)
    line_matrix = jnp.where(mine, held, theirs)

    waves = [trig(ids, stacks[d].astype(F32), omega, d == 1) for d in range(2)]

    keep0, send0, phased, sent = column_solve(ids, messages, line_matrix, waves[0])
    came = lax.ppermute(sent, "freq", swap)
    partner0 = lax.ppermute(send0, "space", flip(space, 1))
    own = column_rest(ids, phased, line_matrix, rows)
    keep1, send1, phased, sent = row_solve(ids, own, came, line_matrix, waves[1], rows)
    came = lax.ppermute(sent, "freq", swap)
    partner1 = lax.ppermute(send1, "space", flip(space, 1))
    own = row_rest(ids, phased, line_matrix)

    solved = last_solve(ids, 0, own, came, line_matrix, rows)
    finals = send(solved, 0, coming)
    solved = last_solve(ids, 1, own, came, line_matrix, rows)
    finals += send(solved, 1, coming)

    sums = []
    for depth, keep, partner in ((0, keep0, partner0), (1, keep1, partner1)):
        stay, away = image_terms(ids, keep, partner, weight, depth == 1)
        sums.append(stay + lax.ppermute(away, "freq", flip(groups, 2)).astype(F32))

    def half_of(v, at, axis):
        return lax.dynamic_index_in_dim(v, at, axis, keepdims=False)

    low, high = z % 2, z // 2
    paired = jnp.stack(sums, axis=1).reshape(2, 2, 2, quarter, half)
    near = lax.ppermute(half_of(paired, 1 - low, 1).astype(BF), "space", flip(space, 2))
    pair = half_of(paired, low, 1) + near.astype(F32)
    far = lax.ppermute(half_of(pair, 1 - high, 0).astype(BF), "space", flip(space, 4))
    piece = (half_of(pair, high, 0) + far.astype(F32)).astype(BF)
    pair = jnp.stack([piece, lax.ppermute(piece, "freq", flip(groups, 2))])
    quad = jnp.stack([pair, lax.ppermute(pair, "freq", swap)], axis=1)

    stay, away = last_term(ids, finals, image_weights)
    chip = (stay + lax.ppermute(away, "freq", swap).astype(F32)).astype(BF)
    both_x = chip.astype(F32) + lax.ppermute(chip, "freq", flip(groups, 2)).astype(F32)
    mine2 = both_x.astype(BF)
    theirs2 = lax.ppermute(mine2, "freq", swap)
    source_out, receiver_out = arrive(ids, finals, freqs)
    return source_out, receiver_out, gradient_rows(ids, quad, mine2, theirs2)


def to_blocks(matrix, pieces):
    leading = matrix.shape[:-2]
    local_rows = matrix.shape[-2]
    columns = matrix.shape[-1] // pieces
    arranged = matrix.reshape(leading + (local_rows, pieces, columns))
    arranged = jnp.moveaxis(arranged, -2, -3)
    return arranged.reshape(leading + (pieces, local_rows * columns))


def from_blocks(blocked, local_rows):
    leading = blocked.shape[:-2]
    pieces = blocked.shape[-2]
    columns = blocked.shape[-1] // local_rows
    arranged = blocked.reshape(leading + (pieces, local_rows, columns))
    arranged = jnp.moveaxis(arranged, -1, -3)
    return arranged.reshape(leading + (columns, pieces * local_rows))


def rotate(fields, phase_angle):
    cosine = jnp.cos(phase_angle)
    sine_part = jnp.sin(phase_angle)
    flip_sign = jnp.array([1.0, -1.0], jnp.float32).reshape(2, 1, 1, 1)
    real_part = fields[:, 0]
    imag_part = fields[:, 1]
    return jnp.stack(
        [
            real_part * cosine + flip_sign * imag_part * sine_part,
            imag_part * cosine - flip_sign * real_part * sine_part,
        ],
        axis=1,
    )


def line_solve(line_inverse, fields):
    flip_sign = jnp.array([1.0, -1.0], jnp.float32).reshape(2, 1, 1, 1)
    prod_real = jnp.einsum(
        "fij,wpfrj->wpfri", line_inverse[0], fields, preferred_element_type=jnp.float32
    )
    prod_imag = jnp.einsum(
        "fij,wpfrj->wpfri", line_inverse[1], fields, preferred_element_type=jnp.float32
    )
    new_real = prod_real[:, 0] - flip_sign * prod_imag[:, 1]
    new_imag = prod_real[:, 1] + flip_sign * prod_imag[:, 0]
    return jnp.stack([new_real, new_imag], axis=1)


def march_step(line_inverse, phased, local_rows):
    pieces = lax.axis_size("space")
    across = line_solve(line_inverse, phased).astype(jnp.bfloat16)
    received = lax.all_to_all(
        to_blocks(across, pieces), "space", split_axis=3, concat_axis=3, tiled=True
    )
    return line_solve(line_inverse, from_blocks(received, local_rows))


def image_slice(fields, image_weights):
    image_term = fields[0, 0] * fields[1, 0] + fields[0, 1] * fields[1, 1]
    return jnp.sum(image_weights[:, None, None] * image_term, axis=0)


def reduce_slice(image_term):
    return lax.psum(image_term.astype(jnp.bfloat16), "freq").astype(jnp.float32)


def finish_sums(slices):
    stacked = jnp.stack(slices)
    return stacked


def general(source_field, receiver_field, line_inverse, lens_delay, omegas, image_weights):
    pieces = lax.axis_size("space")
    local_rows = lens_delay.shape[1]
    depth_count = lens_delay.shape[0]
    wavefields = jnp.stack([source_field, receiver_field]).astype(jnp.float32)
    slices = []
    lens_columns = from_blocks(
        lax.all_to_all(
            to_blocks(lens_delay, pieces), "space", split_axis=1, concat_axis=1, tiled=True
        ),
        local_rows,
    )
    phased = rotate(wavefields, omegas[:, None, None] * lens_delay[0][None]).astype(jnp.bfloat16)
    solved = march_step(line_inverse, phased, local_rows)
    slices.append(reduce_slice(image_slice(solved, image_weights)))
    for depth_step in range(1, depth_count):
        phase_angle = omegas[:, None, None] * lens_columns[depth_step][None]
        phased_columns = rotate(solved, phase_angle).astype(jnp.bfloat16)
        received = lax.all_to_all(
            to_blocks(phased_columns, pieces), "space", split_axis=3, concat_axis=3, tiled=True
        )
        solved = march_step(line_inverse, from_blocks(received, local_rows), local_rows)
        slices.append(reduce_slice(image_slice(solved, image_weights)))
    final_blocks = lax.all_to_all(
        to_blocks(solved.astype(jnp.bfloat16), pieces),
        "space",
        split_axis=3,
        concat_axis=3,
        tiled=True,
    )
    final_fields = from_blocks(final_blocks, local_rows)
    gradient_columns = finish_sums(slices)
    gradient = from_blocks(
        lax.all_to_all(
            to_blocks(gradient_columns, pieces).astype(jnp.bfloat16),
            "space",
            split_axis=1,
            concat_axis=1,
            tiled=True,
        ).astype(jnp.float32),
        local_rows,
    )
    return (final_fields[0], final_fields[1], gradient)


def on_device(source_field, receiver_field, line_inverse, lens_delay, omegas, image_weights):
    args = (source_field, receiver_field, line_inverse, lens_delay, omegas, image_weights)
    groups, space = lax.axis_size("freq"), lax.axis_size("space")
    freqs, depths = omegas.shape[0], lens_delay.shape[0]
    fits = space == 2 * 2 * freqs and freqs == 2 and groups % 4 == 0 and depths == 3
    if not fits:
        return general(*args)
    return plane_per_chip(*args)


def solution(mesh):
    placed = (
        P(None, "freq", "space", None),
        P(None, "freq", "space", None),
        P(None, "freq", None, None),
        P(None, "space", None),
        P("freq"),
        P("freq"),
    )
    return jax.shard_map(
        on_device,
        mesh=mesh,
        in_specs=placed,
        out_specs=(
            P(None, "freq", "space", None),
            P(None, "freq", "space", None),
            P(None, "space", None),
        ),
        check_vma=False,
    )
```

```python
import jax
import jax.numpy as jnp
from jax import lax
from jax.experimental import pallas as pl
from jax.experimental.pallas import tpu as pltpu
from jax.sharding import PartitionSpec as P


BF = jnp.bfloat16
F32 = jnp.float32
CHUNKS = 1
TILES = 2
GRANT = 16
TWO_OVER_PI = 0.63661977236758134
LENS_GAIN = 1.66
ANY = pl.BlockSpec(memory_space=pl.ANY)
SMEM = pl.BlockSpec(memory_space=pltpu.SMEM)


def sin_cos(quarter_turns):
    whole = jnp.round(quarter_turns)
    r = quarter_turns - whole
    q = r * r
    s = -0.00460174 * q + 0.07968794
    s = s * q - 0.64596367
    s = (s * q + 1.57079632) * r
    c = 0.00091925 * q - 0.02086341
    c = c * q + 0.25366950
    c = c * q - 1.23370055
    c = c * q + 1.0
    k = whole.astype(jnp.int32)
    odd = (k & 1) == 1
    sine = jnp.where(odd, c, s)
    cosine = jnp.where(odd, s, c)
    sine = jnp.where((k & 2) == 2, -sine, sine)
    cosine = jnp.where(((k + 1) & 2) == 2, -cosine, cosine)
    return sine, cosine


def dot_rows(a, b):
    return lax.dot_general(a, b, (((1,), (0,)), ((), ())), preferred_element_type=F32)


def dot_lines(a, b):
    return lax.dot_general(a, b, (((1,), (1,)), ((), ())), preferred_element_type=F32)


def spec(block, index):
    return pl.BlockSpec(block, index)


def call(body, grid, ins, outs, scratch, operands, cost, limit=28 << 20):
    return pl.pallas_call(
        body,
        out_shape=[jax.ShapeDtypeStruct(s, d) for s, d, _, _ in outs],
        grid_spec=pltpu.PrefetchScalarGridSpec(
            num_scalar_prefetch=1,
            grid=grid,
            in_specs=ins,
            out_specs=[pl.BlockSpec(b, i) for _, _, b, i in outs],
            scratch_shapes=scratch,
        ),
        compiler_params=pltpu.CompilerParams(vmem_limit_bytes=limit),
        cost_estimate=pl.CostEstimate(flops=cost, bytes_accessed=8 << 20, transcendentals=0),
    )(*operands)


VMEM = pl.BlockSpec(memory_space=pltpu.VMEM)


def solid(body, outs, scratch, operands, cost, limit, ins=None):
    return pl.pallas_call(
        body,
        out_shape=[jax.ShapeDtypeStruct(s, d) for s, d in outs],
        in_specs=[SMEM] + (ins or [VMEM] * (len(operands) - 1)),
        out_specs=[VMEM] * len(outs),
        scratch_shapes=scratch,
        compiler_params=pltpu.CompilerParams(vmem_limit_bytes=limit << 20),
        cost_estimate=pl.CostEstimate(flops=cost, bytes_accessed=8 << 20, transcendentals=0),
    )(*operands)


def home_solve(ids, turn, source, receiver, matrix, lens, omegas):
    _, _, rows, cols = source.shape
    half = cols // 2

    def body(ids, src, rec, mat, len_ref, om, m00, m01, m10, m11, phased):
        b = pl.program_id(0)
        y = ids[3]
        j = ids[4] ^ turn

        @pl.when(b == 0)
        def _():
            sine, cosine = sin_cos(len_ref[0] * (om[j] * TWO_OVER_PI))
            sr = src[0, 0].astype(F32)
            si = src[1, 0].astype(F32)
            rr = rec[0, 0].astype(F32)
            ri = -rec[1, 0].astype(F32)
            first = y == 0
            for at, (re, im) in enumerate(
                (
                    (jnp.where(first, sr, rr), jnp.where(first, si, ri)),
                    (jnp.where(first, rr, sr), jnp.where(first, ri, si)),
                )
            ):
                phased[pl.ds(at * rows, rows), :] = (re * cosine + im * sine).astype(BF)
                phased[pl.ds((2 + at) * rows, rows), :] = (im * cosine - re * sine).astype(BF)

        q_re = dot_lines(phased[...], mat[0, 0])
        q_im = dot_lines(phased[...], mat[1, 0])
        n = 2 * rows
        new_re = (q_re[:n] - q_im[n:]).astype(BF)
        new_im = (q_re[n:] + q_im[:n]).astype(BF)
        for at, outs in enumerate(((m00, m10), (m01, m11))):

            @pl.when(b == at)
            def _(outs=outs):
                for w, out in enumerate(outs):
                    out[0] = new_re[w * rows : (w + 1) * rows]
                    out[1] = new_im[w * rows : (w + 1) * rows]

    message = ((2, rows, half), BF, (2, rows, half), lambda b, ids: (0, 0, 0))
    field = spec((2, 1, rows, cols), lambda b, ids: (0, ids[4] ^ turn, 0, 0))
    return call(
        body,
        (2,),
        [
            field,
            field,
            spec((2, 1, half, cols), lambda b, ids: (0, ids[4] ^ turn, ids[5] ^ b, 0)),
            spec((1, rows, cols), lambda b, ids: (0, 0, 0)),
            SMEM,
        ],
        [message] * 4,
        [pltpu.VMEM((4 * rows, cols), BF)],
        (ids, source, receiver, matrix, lens, omegas),
        2 * 4 * rows * cols * cols * 2,
        60 << 20,
    )


def trig(ids, stack, omega, by_rows):
    _, quarter, half = stack.shape
    slices = stack.shape[0] // 2
    rows, cols = (quarter, 2 * half) if by_rows else (2 * quarter, half)

    def body(ids, pieces, om, sine_ref, cosine_ref):
        s = pl.program_id(0)
        for side in range(2):
            x_at, y_at = ids[1] ^ side, ids[3] ^ (s % 2)
            at = (x_at * 2 + y_at) * 4 + (ids[2] ^ (s // 2))
            sine, cosine = sin_cos(pieces[at] * (om[0] * (TWO_OVER_PI / LENS_GAIN)))
            if by_rows:
                to = (slice(None), pl.ds(side * half, half))
            else:
                to = (pl.ds(side * quarter, quarter), slice(None))
            sine_ref[to] = sine
            cosine_ref[to] = cosine

    out = ((slices * rows, cols), F32, (rows, cols), lambda s, ids: (s, 0))
    return call(
        body,
        (slices,),
        [spec(stack.shape, lambda s, ids: (0, 0, 0)), SMEM],
        [out, out],
        [],
        (ids, stack, omega),
        1 << 26,
        12 << 20,
    )


def rotated(re, im, sine, cosine):
    return (re * cosine + im * sine).astype(BF), (im * cosine - re * sine).astype(BF)


def column_solve(ids, messages, matrix, waves):
    _, rows, half = messages[0].shape
    n = matrix.shape[-1]
    slices = n // rows
    tile = n // TILES
    chunk = half // CHUNKS
    quarter = rows // 2
    blocked = matrix.reshape(2, slices, 2, quarter, n)

    def body(ids, *refs):
        ms, (mat, sine_ref, cosine_ref, keep, send, phased, out, field) = refs[:8], refs[8:]
        t = ids[4] * 2 + ids[3]
        for at, m in enumerate(ms):
            a, b = at // 2, at % 2
            place = (ids[0] ^ b) * 4 + (t ^ a)
            to = pl.ds(pl.multiple_of(place * rows, rows), rows)
            field[0, to] = m[0]
            field[1, to] = m[1]
        first = ids[3] == 0
        for i in range(TILES):
            per = tile // rows
            left = mat[:, i * per : (i + 1) * per].reshape(2 * tile, n)
            to = pl.ds(i * tile, tile)
            for c in range(CHUNKS):
                cols = pl.ds(c * chunk, chunk)
                q_re = dot_rows(left, field[0, :, cols])
                q_im = dot_rows(left, field[1, :, cols])
                new_re = q_re[:tile] - q_im[tile:]
                new_im = q_im[:tile] + q_re[tile:]
                re, im = rotated(new_re, new_im, sine_ref[to, cols], cosine_ref[to, cols])
                phased[0, to, cols] = re
                phased[1, to, cols] = im
                for part, new in enumerate((new_re, new_im)):
                    for line in range(per // 2):
                        lo = 2 * line * rows
                        even = new[lo : lo + rows].astype(BF)
                        odd = new[lo + rows : lo + 2 * rows].astype(BF)
                        z = i * (per // 2) + line
                        keep[part, z, :, cols] = jnp.where(first, even, odd)
                        send[part, z, :, cols] = jnp.where(first, odd, even)
        column_half(mat, 1 - ids[0], phased, out)

    part = ((2, slices // 2, rows, half), BF)
    return solid(
        body,
        [part, part, ((2, n, half), BF), ((2, n // 2, half), BF)],
        [pltpu.VMEM((2, n, half), BF)],
        (ids, *messages, blocked, *waves),
        12 * n * n * half,
        GRANT,
    )


def column_half(mat, side, field, out):
    _, _, _, _, n = mat.shape
    tile = n // 2
    half = field.shape[-1]
    chunk = half // CHUNKS
    left = mat[:, :, side].reshape(2 * tile, n)
    for c in range(CHUNKS):
        cols = pl.ds(c * chunk, chunk)
        q_re = dot_rows(left, field[0, :, cols])
        q_im = dot_rows(left, field[1, :, cols])
        out[0, :, cols] = (q_re[:tile] - q_im[tile:]).astype(BF)
        out[1, :, cols] = (q_im[:tile] + q_re[tile:]).astype(BF)


def column_rest(ids, phased, matrix, rows):
    _, n, half = phased.shape
    blocked = matrix.reshape(2, n // rows, 2, rows // 2, n)

    def body(ids, field, mat, out):
        column_half(mat, ids[0], field, out)

    return solid(
        body,
        [((2, n // 2, half), BF)],
        [],
        (ids, phased, blocked),
        4 * n * n * half,
        GRANT,
    )[0]


def row_solve(ids, own, received, matrix, waves, rows):
    _, lines, half = own.shape
    n = matrix.shape[-1]
    slices = n // rows
    quarter = rows // 2
    tile = n // TILES

    def body(ids, own_ref, rec_ref, mat, sine_ref, cosine_ref, keep, send, phased, out, field):
        for at, ref in enumerate((own_ref, rec_ref)):
            to = pl.ds(pl.multiple_of((ids[0] ^ at) * half, half), half)
            field[pl.ds(0, lines), to] = ref[0]
            field[pl.ds(lines, lines), to] = ref[1]
        first = ids[3] == 0
        for i in range(TILES * CHUNKS):
            cols = pl.ds(i * (tile // CHUNKS), tile // CHUNKS)
            q_re = dot_lines(field[...], mat[0, cols])
            q_im = dot_lines(field[...], mat[1, cols])
            new_re = q_re[:lines] - q_im[lines:]
            new_im = q_re[lines:] + q_im[:lines]
            re, im = rotated(new_re, new_im, sine_ref[:, cols], cosine_ref[:, cols])
            phased[0, :, cols] = re
            phased[1, :, cols] = im
            for part, new in enumerate((new_re, new_im)):
                for z in range(slices // 2):
                    lo = 2 * z * quarter
                    even = new[lo : lo + quarter].astype(BF)
                    odd = new[lo + quarter : lo + 2 * quarter].astype(BF)
                    keep[part, z, :, cols] = jnp.where(first, even, odd)
                    send[part, z, :, cols] = jnp.where(first, odd, even)
        row_half(mat, 1 - ids[0], phased, out)

    part = ((2, slices // 2, quarter, n), BF)
    return solid(
        body,
        [part, part, ((2, lines, n), BF), ((2, lines, half), BF)],
        [pltpu.VMEM((2 * lines, n), BF)],
        (ids, own, received, matrix, *waves),
        12 * n * n * half,
        GRANT,
    )


def row_half(mat, side, field, out):
    _, lines, n = field.shape
    half = n // 2
    chunk = half // CHUNKS
    left = field[...].reshape(2 * lines, n)
    for c in range(CHUNKS):
        at = pl.ds(pl.multiple_of(side * half + c * chunk, chunk), chunk)
        q_re = dot_lines(left, mat[0, at])
        q_im = dot_lines(left, mat[1, at])
        cols = pl.ds(c * chunk, chunk)
        out[0, :, cols] = (q_re[:lines] - q_im[lines:]).astype(BF)
        out[1, :, cols] = (q_re[lines:] + q_im[:lines]).astype(BF)


def row_rest(ids, phased, matrix):
    _, lines, n = phased.shape

    def body(ids, field, mat, out):
        row_half(mat, ids[0], field, out)

    return solid(
        body,
        [((2, lines, n // 2), BF)],
        [],
        (ids, phased, matrix),
        4 * n * n * (n // 2),
        GRANT,
    )[0]


def last_solve(ids, turn, own, received, matrix, rows):
    _, _, half = own.shape
    n = matrix.shape[-1]
    slices = n // rows
    quarter = rows // 2

    def body(ids, own_ref, rec_ref, mat, m00, m01, m10, m11, field):
        for at, ref in enumerate((own_ref, rec_ref)):
            side = (ids[0] ^ at) * quarter
            for part in range(2):
                for s in range(slices):
                    to = pl.ds(pl.multiple_of(s * rows + side, quarter), quarter)
                    field[part, to] = ref[part, pl.ds(s * quarter, quarter)]
        outs = (m00, m01, m10, m11)
        left = []
        for part in range(2):
            for at in range(4):
                s = (ids[0] ^ (at % 2)) * 4 + (ids[4] ^ (at // 2)) * 2 + (ids[3] ^ turn)
                left.append(mat[part, pl.ds(pl.multiple_of(s * rows, rows), rows)])
        left = jnp.concatenate(left)
        q_re = dot_rows(left, field[0])
        q_im = dot_rows(left, field[1])
        n_rows = 4 * rows
        new_re = (q_re[:n_rows] - q_im[n_rows:]).astype(BF)
        new_im = q_im[:n_rows] + q_re[n_rows:]
        new_im = jnp.where(ids[3] == 0, new_im, -new_im).astype(BF)
        for at, out in enumerate(outs):
            out[0] = new_re[at * rows : (at + 1) * rows]
            out[1] = new_im[at * rows : (at + 1) * rows]

    return solid(
        body,
        [((2, rows, half), BF)] * 4,
        [pltpu.VMEM((2, n, half), BF)],
        (ids, own, received, matrix),
        4 * n * n * half,
        GRANT,
    )


def last_term(ids, messages, image_weights):
    _, rows, half = messages[0].shape
    high = rows // 2

    def body(ids, *refs):
        ms, (wt, stay, away) = refs[:8], refs[8:]
        sides = []
        for b in range(2):
            total = None
            for turn in range(2):
                s, r = ms[4 * turn + b], ms[4 * turn + 2 + b]
                term = s[0].astype(F32) * r[0].astype(F32) + s[1].astype(F32) * r[1].astype(F32)
                term = wt[ids[4] ^ turn] * term
                total = term if total is None else total + term
            sides.append(total)
        left = ids[5] == 0
        for b in range(2):
            value = jnp.where(left, sides[b], sides[1 - b])
            lo, hi = value[:high], value[high:]
            first = ids[0] == 0
            cols = pl.ds(b * half, half)
            stay[:, cols] = jnp.where(first, lo, hi)
            away[:, cols] = jnp.where(first, hi, lo).astype(BF)

    shape = (high, 2 * half)
    index = lambda i, ids: (0, 0)
    return call(
        body,
        (1,),
        [spec((2, rows, half), lambda i, ids: (0, 0, 0))] * 8 + [SMEM],
        [(shape, F32, shape, index), (shape, BF, shape, index)],
        [],
        (ids, *messages, image_weights),
        1 << 22,
        14 << 20,
    )


def arrive(ids, messages, freqs):
    _, rows, half = messages[0].shape

    def body(ids, *refs):
        ms, (src, rec, held, sems) = refs[:8], refs[8:]
        copies = [
            pltpu.make_async_copy(m, held.at[at], sems.at[at]) for at, m in enumerate(ms)
        ]
        for copy in copies:
            copy.start()
        for copy in copies:
            copy.wait()
        for side in range(2):
            for j in range(freqs):
                a_hi = ids[4] ^ j
                b = ids[5] ^ side
                cols = pl.ds(side * half, half)
                src[:, j, :, cols] = held[(a_hi * 2 + ids[3]) * 2 + b]
                rec[:, j, :, cols] = held[(a_hi * 2 + (1 - ids[3])) * 2 + b]

    full = (2, freqs, rows, 2 * half)
    index = lambda i, ids: (0, 0, 0, 0)
    return call(
        body,
        (1,),
        [ANY] * 8,
        [(full, BF, full, index), (full, BF, full, index)],
        [pltpu.VMEM((8, 2, rows, half), BF), pltpu.SemaphoreType.DMA((8,))],
        (ids, *messages),
        1 << 22,
        12 << 20,
    )


def image_terms(ids, keep, other, weight, by_rows):
    _, lines, rows, cols = keep.shape
    high, wide = (rows, cols // 2) if by_rows else (rows // 2, cols)

    def body(ids, k, o, wt, stay, away):
        first = ids[1] == 0
        re = k[0, 0].astype(F32) * o[0, 0].astype(F32)
        term = wt[0] * (re - k[1, 0].astype(F32) * o[1, 0].astype(F32))
        lo, hi = (term[:, :wide], term[:, wide:]) if by_rows else (term[:high], term[high:])
        stay[0] = jnp.where(first, lo, hi)
        away[0] = jnp.where(first, hi, lo).astype(BF)

    block = spec((2, 1, rows, cols), lambda i, ids: (0, i, 0, 0))
    shape, piece = (lines, high, wide), (1, high, wide)
    index = lambda i, ids: (i, 0, 0)
    return call(
        body,
        (lines,),
        [block, block, SMEM],
        [(shape, F32, piece, index), (shape, BF, piece, index)],
        [],
        (ids, keep, other, weight),
        1 << 22,
        8 << 20,
    )


def gradient_rows(ids, quad, mine, theirs):
    quarter, half = quad.shape[-2:]
    rows, cols = 2 * quarter, 2 * half

    def body(ids, quad_ref, mine_ref, theirs_ref, out):
        for a in range(2):
            for b in range(2):
                to = (pl.ds(a * quarter, quarter), pl.ds(b * half, half))
                out[(0, *to)] = quad_ref[ids[1] ^ a, ids[0] ^ b, 0].astype(F32)
                out[(1, *to)] = quad_ref[ids[1] ^ b, ids[0] ^ a, 1].astype(F32)
        first = ids[0] == 0
        own, other = mine_ref[...].astype(F32), theirs_ref[...].astype(F32)
        out[2, pl.ds(0, quarter)] = jnp.where(first, own, other)
        out[2, pl.ds(quarter, quarter)] = jnp.where(first, other, own)

    flat = lambda rank: (lambda i, ids: (0,) * rank)
    full = (3, rows, cols)
    return call(
        body,
        (1,),
        [spec(quad.shape, flat(5)), spec(mine.shape, flat(2)), spec(mine.shape, flat(2))],
        [(full, F32, full, flat(3))],
        [],
        (ids, quad, mine, theirs),
        1 << 20,
        8 << 20,
    )[0]


def flip(size, bit):
    return [(i, i ^ bit) for i in range(size)]


def scatter_rounds(groups, space, back):
    rounds = []
    for a in range(4):
        for b in range(2):
            perm = []
            for x in range(groups // 2):
                for c in range(2):
                    for s in range(space):
                        home = (2 * x + c) * space + s
                        away = (2 * x + ((s // 4) ^ b)) * space + 4 * c + ((s % 4) ^ a)
                        perm.append((away, home) if back else (home, away))
            rounds.append(perm)
    return rounds


def plane_per_chip(source, receiver, matrix, lens, omegas, image_weights):
    groups, space = lax.axis_size("freq"), lax.axis_size("space")
    both = ("freq", "space")
    _, freqs, rows, cols = source.shape
    half, quarter = cols // 2, rows // 2
    group, s = lax.axis_index("freq"), lax.axis_index("space")
    core, x, z, y = group % 2, group // 2, s // 2, s % 2
    ids = jnp.stack([core, x, z, y, z % 2, z // 2]).astype(jnp.int32)
    swap = flip(groups, 1)

    going, coming = scatter_rounds(groups, space, False), scatter_rounds(groups, space, True)

    def send(outputs, turn, rounds):
        return [lax.ppermute(m, both, rounds[4 * turn + at]) for at, m in enumerate(outputs)]

    corners = ((1, x * quarter, core * half), (2, core * quarter, x * half))
    piece = jnp.concatenate(
        [lax.dynamic_slice(lens, corner, (1, quarter, half)) for corner in corners]
    )
    piece = (piece * LENS_GAIN).astype(jnp.float16)
    line = [piece] + [lax.ppermute(piece, "space", flip(space, 2 * k)) for k in (1, 2, 3)]
    line = jnp.stack(line, axis=1)
    other_line = lax.ppermute(line, "space", flip(space, 1))
    planes = [jnp.concatenate([line[d], other_line[d]]) for d in range(2)]
    stacks = [
        jnp.concatenate([planes[d], lax.ppermute(planes[d], "freq", flip(groups, 2))])
        for d in range(2)
    ]

    solved = home_solve(ids, 0, source, receiver, matrix, lens, omegas)
    messages = send(solved, 0, going)
    solved = home_solve(ids, 1, source, receiver, matrix, lens, omegas)
    messages += send(solved, 1, going)

    mine = core == z // 2
    scalars = jnp.stack([omegas, image_weights])
    other = lax.ppermute(scalars, "freq", swap)
    omega, weight = jnp.where(mine, scalars, other)[:, z % 2]
    omega, weight = omega.reshape(1), weight.reshape(1)
    held = lax.dynamic_slice(matrix, (0, z % 2, 0, 0), (2, 1, cols, cols))[:, 0]
    theirs = lax.ppermute(held, "freq", swap)
    line_matrix = jnp.where(mine, held, theirs)

    waves = [trig(ids, stacks[d].astype(F32), omega, d == 1) for d in range(2)]

    keep0, send0, phased, sent = column_solve(ids, messages, line_matrix, waves[0])
    came = lax.ppermute(sent, "freq", swap)
    partner0 = lax.ppermute(send0, "space", flip(space, 1))
    own = column_rest(ids, phased, line_matrix, rows)
    keep1, send1, phased, sent = row_solve(ids, own, came, line_matrix, waves[1], rows)
    came = lax.ppermute(sent, "freq", swap)
    partner1 = lax.ppermute(send1, "space", flip(space, 1))
    own = row_rest(ids, phased, line_matrix)

    finals = [None] * 8
    for turn in range(2):
        solved = last_solve(ids, turn, own, came, line_matrix, rows)
        for at, m in enumerate(solved):
            place = (at // 2) * 4 + turn * 2 + at % 2
            finals[place] = lax.ppermute(m, both, coming[place])

    def half_of(v, at, axis):
        return lax.dynamic_index_in_dim(v, at, axis, keepdims=False)

    low, high = z % 2, z // 2
    pieces = []
    for depth, keep, partner in ((0, keep0, partner0), (1, keep1, partner1)):
        stay, away = image_terms(ids, keep, partner, weight, depth == 1)
        over_x = stay + lax.ppermute(away, "freq", flip(groups, 2)).astype(F32)
        paired = over_x.reshape(2, 2, quarter, half)
        near = half_of(paired, 1 - low, 1).astype(BF)
        near = lax.ppermute(near, "space", flip(space, 2))
        pair = half_of(paired, low, 1) + near.astype(F32)
        far = half_of(pair, 1 - high, 0).astype(BF)
        far = lax.ppermute(far, "space", flip(space, 4))
        piece = (half_of(pair, high, 0) + far.astype(F32)).astype(BF)
        pieces.append(jnp.stack([piece, lax.ppermute(piece, "freq", flip(groups, 2))]))
    pair = jnp.stack(pieces, axis=1)
    quad = jnp.stack([pair, lax.ppermute(pair, "freq", swap)], axis=1)

    stay, away = last_term(ids, finals, image_weights)
    chip = (stay + lax.ppermute(away, "freq", swap).astype(F32)).astype(BF)
    both_x = chip.astype(F32) + lax.ppermute(chip, "freq", flip(groups, 2)).astype(F32)
    mine2 = both_x.astype(BF)
    theirs2 = lax.ppermute(mine2, "freq", swap)
    source_out, receiver_out = arrive(ids, finals, freqs)
    return source_out, receiver_out, gradient_rows(ids, quad, mine2, theirs2)


def to_blocks(matrix, pieces):
    leading = matrix.shape[:-2]
    local_rows = matrix.shape[-2]
    columns = matrix.shape[-1] // pieces
    arranged = matrix.reshape(leading + (local_rows, pieces, columns))
    arranged = jnp.moveaxis(arranged, -2, -3)
    return arranged.reshape(leading + (pieces, local_rows * columns))


def from_blocks(blocked, local_rows):
    leading = blocked.shape[:-2]
    pieces = blocked.shape[-2]
    columns = blocked.shape[-1] // local_rows
    arranged = blocked.reshape(leading + (pieces, local_rows, columns))
    arranged = jnp.moveaxis(arranged, -1, -3)
    return arranged.reshape(leading + (columns, pieces * local_rows))


def rotate(fields, phase_angle):
    cosine = jnp.cos(phase_angle)
    sine_part = jnp.sin(phase_angle)
    flip_sign = jnp.array([1.0, -1.0], jnp.float32).reshape(2, 1, 1, 1)
    real_part = fields[:, 0]
    imag_part = fields[:, 1]
    return jnp.stack(
        [
            real_part * cosine + flip_sign * imag_part * sine_part,
            imag_part * cosine - flip_sign * real_part * sine_part,
        ],
        axis=1,
    )


def line_solve(line_inverse, fields):
    flip_sign = jnp.array([1.0, -1.0], jnp.float32).reshape(2, 1, 1, 1)
    prod_real = jnp.einsum(
        "fij,wpfrj->wpfri", line_inverse[0], fields, preferred_element_type=jnp.float32
    )
    prod_imag = jnp.einsum(
        "fij,wpfrj->wpfri", line_inverse[1], fields, preferred_element_type=jnp.float32
    )
    new_real = prod_real[:, 0] - flip_sign * prod_imag[:, 1]
    new_imag = prod_real[:, 1] + flip_sign * prod_imag[:, 0]
    return jnp.stack([new_real, new_imag], axis=1)


def march_step(line_inverse, phased, local_rows):
    pieces = lax.axis_size("space")
    across = line_solve(line_inverse, phased).astype(jnp.bfloat16)
    received = lax.all_to_all(
        to_blocks(across, pieces), "space", split_axis=3, concat_axis=3, tiled=True
    )
    return line_solve(line_inverse, from_blocks(received, local_rows))


def image_slice(fields, image_weights):
    image_term = fields[0, 0] * fields[1, 0] + fields[0, 1] * fields[1, 1]
    return jnp.sum(image_weights[:, None, None] * image_term, axis=0)


def reduce_slice(image_term):
    return lax.psum(image_term.astype(jnp.bfloat16), "freq").astype(jnp.float32)


def finish_sums(slices):
    stacked = jnp.stack(slices)
    return stacked


def general(source_field, receiver_field, line_inverse, lens_delay, omegas, image_weights):
    pieces = lax.axis_size("space")
    local_rows = lens_delay.shape[1]
    depth_count = lens_delay.shape[0]
    wavefields = jnp.stack([source_field, receiver_field]).astype(jnp.float32)
    slices = []
    lens_columns = from_blocks(
        lax.all_to_all(
            to_blocks(lens_delay, pieces), "space", split_axis=1, concat_axis=1, tiled=True
        ),
        local_rows,
    )
    phased = rotate(wavefields, omegas[:, None, None] * lens_delay[0][None]).astype(jnp.bfloat16)
    solved = march_step(line_inverse, phased, local_rows)
    slices.append(reduce_slice(image_slice(solved, image_weights)))
    for depth_step in range(1, depth_count):
        phase_angle = omegas[:, None, None] * lens_columns[depth_step][None]
        phased_columns = rotate(solved, phase_angle).astype(jnp.bfloat16)
        received = lax.all_to_all(
            to_blocks(phased_columns, pieces), "space", split_axis=3, concat_axis=3, tiled=True
        )
        solved = march_step(line_inverse, from_blocks(received, local_rows), local_rows)
        slices.append(reduce_slice(image_slice(solved, image_weights)))
    final_blocks = lax.all_to_all(
        to_blocks(solved.astype(jnp.bfloat16), pieces),
        "space",
        split_axis=3,
        concat_axis=3,
        tiled=True,
    )
    final_fields = from_blocks(final_blocks, local_rows)
    gradient_columns = finish_sums(slices)
    gradient = from_blocks(
        lax.all_to_all(
            to_blocks(gradient_columns, pieces).astype(jnp.bfloat16),
            "space",
            split_axis=1,
            concat_axis=1,
            tiled=True,
        ).astype(jnp.float32),
        local_rows,
    )
    return (final_fields[0], final_fields[1], gradient)


def on_device(source_field, receiver_field, line_inverse, lens_delay, omegas, image_weights):
    args = (source_field, receiver_field, line_inverse, lens_delay, omegas, image_weights)
    groups, space = lax.axis_size("freq"), lax.axis_size("space")
    freqs, depths = omegas.shape[0], lens_delay.shape[0]
    fits = space == 2 * 2 * freqs and freqs == 2 and groups % 4 == 0 and depths == 3
    if not fits:
        return general(*args)
    return plane_per_chip(*args)


def solution(mesh):
    placed = (
        P(None, "freq", "space", None),
        P(None, "freq", "space", None),
        P(None, "freq", None, None),
        P(None, "space", None),
        P("freq"),
        P("freq"),
    )
    return jax.shard_map(
        on_device,
        mesh=mesh,
        in_specs=placed,
        out_specs=(
            P(None, "freq", "space", None),
            P(None, "freq", "space", None),
            P(None, "space", None),
        ),
        check_vma=False,
    )
```
